32 devices in a mesh: gx: 4 (over y, core), gy: 8 (over z, x).
Axes of the slice: x: 2, y: 2, z: 4, core: 2. Of those that a mesh axis runs over, the one named last changes fastest.
Arguments:
- orbitals: bfloat16 [56, 56, 29, 256], P('gx', 'gy'), may hold values from -6 to 6
- cell_matrices: bfloat16 [4, 8, 8, 512, 512], P('gx', 'gy'), may hold values from -0.09375 to 0.09375
- cell_nodes: int32 [4, 8, 8, 512], P('gx', 'gy'), may hold values from 0 to 3479, as said below
- projectors: bfloat16 [4, 8, 8, 16, 32, 512], P('gx', 'gy'), may hold values from -0.125 to 0.125
- entry_atom: int32 [4, 8, 8, 16], P('gx', 'gy'), may hold values from 0 to 1023, as said below
- coupling: float32 [1024, 32, 32], P(('gx', 'gy')), may hold values from -0.75 to 0.75
- proj_counts: int32 [1024], P(('gx', 'gy')), may hold values from 8 to 32
Outputs:
- filtered: bfloat16 [56, 56, 29, 256], P('gx', 'gy')
The draws below stay inside these ranges and needn't reach their ends.
Inputs may be any that keep to these rules, and one draw needn't show every extreme that they name: `cell_nodes`: values index the device's extended node grid of (15) x (8) x (29) nodes, first index slowest; local cell c = i * 4 + l (with j = 0, since each device has one cell along the second direction) names each node of its block of (8) cubed nodes starting at (7 * i, 7 * j, 7 * l) once, in a drawn order. `entry_atom`: atom a is homed on device a // 32, devices numbered over gx and gy with gx slowest. The entries of one device name atoms of any one home device at most 8 times, and exactly 8 times for some home device.
All inputs are finite; a program needn't handle non-finite values.
Results may differ from the reference program's by a relative error of at most 0.0095.
Values may be sent and summed in bfloat16 or wider, within the bound.
No kernel may reach another device: no remote copies, remote signals or barrier semaphores. Data moves between devices by JAX's collectives and lax.ppermute only.
A program may use at most 128 MiB of HBM per device.

```python
import jax
import jax.numpy as jnp
from jax import lax

DEG = 7
CELL_NODES = 512
CX = 2
CY = 1
CZ = 4
CELLS_DEV = 8
ORB = 256
NPROJ = 32
ENT_CELL = 16
E_DEV = 128
ATOM_DEV = 32
ATOMS = 1024
SLOT = 8
FILTER_DEGREE = 3
N_GX = 4
N_GY = 8


def draw_cell_nodes(key, part):
    per_side = DEG + 1
    layers = DEG * CZ + 1
    span_y = DEG * CY + 1
    cell_ids = jnp.arange(CELLS_DEV, dtype=jnp.int32)
    cell_first = cell_ids // (CY * CZ)
    cell_second = cell_ids // CZ % CY
    cell_third = cell_ids % CZ
    node_ids = jnp.arange(CELL_NODES, dtype=jnp.int32)
    node_first = node_ids // (per_side * per_side)
    node_second = node_ids // per_side % per_side
    node_third = node_ids % per_side
    layout = (DEG * cell_first[:, None] + node_first[None, :]) * span_y
    layout = (layout + DEG * cell_second[:, None] + node_second[None, :]) * layers
    layout = layout + DEG * cell_third[:, None] + node_third[None, :]
    subkeys = jax.random.split(jax.random.fold_in(key, 11), N_GX * N_GY * CELLS_DEV)

    def permute_cell(subkey):
        return jax.random.permutation(subkey, CELL_NODES)
    orders = jax.vmap(permute_cell)(subkeys).reshape(N_GX, N_GY, CELLS_DEV, CELL_NODES)
    spread = jnp.broadcast_to(layout, (N_GX, N_GY, CELLS_DEV, CELL_NODES))
    return jnp.take_along_axis(spread, orders, axis=3).astype(jnp.int32)


def draw_entry_atom(key, part):
    slot_total = N_GX * N_GY * SLOT

    def one_device(subkey):
        first_key, second_key, third_key = jax.random.split(subkey, 3)
        shuffled = jax.random.permutation(first_key, slot_total).astype(jnp.int32)
        position = jnp.argsort(shuffled, stable=True).astype(jnp.int32)
        slot_ids = jnp.arange(slot_total, dtype=jnp.int32)
        favoured = shuffled[0] // SLOT
        priority = jnp.where(slot_ids // SLOT == favoured, slot_ids % SLOT - SLOT, position)
        chosen = jnp.argsort(priority, stable=True)[:E_DEV].astype(jnp.int32)
        mixing = jax.random.permutation(second_key, E_DEV)
        homes = chosen[mixing] // SLOT
        within = jax.random.randint(third_key, (E_DEV,), 0, ATOM_DEV)
        return (homes * ATOM_DEV + within).astype(jnp.int32)
    subkeys = jax.random.split(jax.random.fold_in(key, 7), N_GX * N_GY)
    return jax.vmap(one_device)(subkeys).reshape(N_GX, N_GY, CELLS_DEV, ENT_CELL)


def plant(values, stream_key, smallest, largest):
    longest = values.shape.index(max(values.shape))
    spots = []
    for shift in (0, 1):
        where = [jax.random.randint(jax.random.fold_in(stream_key, axis), (), 0, length) for axis, length in enumerate(values.shape)]
        where[longest] = (where[longest] + shift) % values.shape[longest]
        spots.append(tuple(where))
    return values.at[spots[0]].set(smallest).at[spots[1]].set(largest)


def shard_levels(rng, dims, cuts, least, top_value):
    def one(dim, parts):
        steps = jax.random.uniform(jax.random.fold_in(jax.random.fold_in(rng, 6), dim), (parts,), jnp.float32, least / len(cuts), top_value / len(cuts))
        return jnp.repeat(jnp.exp(steps), dims[dim] // parts).reshape((-1,) + (1,) * (len(dims) - dim - 1))

    loudness = one(*cuts[0])
    for cut in cuts[1:]:
        loudness = loudness * one(*cut)
    return loudness


def scatter_about(key, extent, deviation, limit, pieces=(), kind=jnp.bfloat16):
    entries = deviation * jax.random.normal(key, extent, jnp.float32)
    if pieces:
        entries = entries * shard_levels(key, extent, pieces, -0.22, 0.18)
    return jnp.clip(entries, -limit, limit).astype(kind)


def setup_inputs(seed: int = 0) -> dict:
    arg_keys = jax.random.split(jax.random.key(seed), 8)
    return {
        "orbitals": scatter_about(arg_keys[0], (DEG * CX * N_GX, DEG * CY * N_GY, DEG * CZ + 1, ORB), 1.0, 6.0, ((0, 4), (1, 8))),
        "cell_matrices": scatter_about(arg_keys[1], (N_GX, N_GY, CELLS_DEV, CELL_NODES, CELL_NODES), (8 * CELL_NODES) ** -0.5, 0.09375, ((0, 4), (1, 8))),
        "cell_nodes": draw_cell_nodes(jax.random.fold_in(arg_keys[7], 71), 0),
        "projectors": scatter_about(arg_keys[3], (N_GX, N_GY, CELLS_DEV, ENT_CELL, NPROJ, CELL_NODES), (4 * CELL_NODES) ** -0.5, 0.125, ((0, 4), (1, 8))),
        "entry_atom": draw_entry_atom(jax.random.fold_in(arg_keys[7], 71), 0),
        "coupling": scatter_about(arg_keys[5], (ATOMS, NPROJ, NPROJ), (2 * NPROJ) ** -0.5, 0.75, ((0, 32),), jnp.float32),
        "proj_counts": plant(jax.random.randint(arg_keys[6], (ATOMS,), NPROJ // 4, NPROJ + 1), jax.random.fold_in(arg_keys[6], 1), NPROJ // 4, NPROJ).astype(jnp.int32),
    }


def reference(orbitals, cell_matrices, cell_nodes, projectors, entry_atom, coupling, proj_counts):
    span_x = DEG * CX
    span_y = DEG * CY
    layers = DEG * CZ + 1
    global_x = span_x * N_GX
    global_y = span_y * N_GY
    devices = N_GX * N_GY
    index_x = jnp.arange(N_GX, dtype=jnp.int32)[:, None, None, None]
    index_y = jnp.arange(N_GY, dtype=jnp.int32)[None, :, None, None]
    node_z = cell_nodes % layers
    node_y = (cell_nodes // layers) % (span_y + 1)
    node_x = cell_nodes // (layers * (span_y + 1))
    place_x = (index_x * span_x + node_x) % global_x
    place_y = (index_y * span_y + node_y) % global_y
    global_ids = ((place_x * global_y + place_y) * layers + node_z).astype(jnp.int32)
    global_ids = global_ids.reshape(devices, CELLS_DEV, CELL_NODES)
    matrices = cell_matrices.reshape(devices, CELLS_DEV, CELL_NODES, CELL_NODES)
    shapes = projectors.reshape(devices, CELLS_DEV, ENT_CELL, NPROJ, CELL_NODES)
    atom_list = entry_atom.reshape(-1).astype(jnp.int32)
    active = (jnp.arange(NPROJ, dtype=jnp.int32)[None, :] < proj_counts[:, None]).astype(jnp.float32)
    total_rows = global_x * global_y * layers

    def operate(field):
        def project(inputs):
            node_ids, shape_block = inputs
            local = field[node_ids].astype(jnp.float32)
            return jnp.einsum("ckpn,cno->ckpo", shape_block.astype(jnp.float32), local).astype(jnp.bfloat16)

        projected = lax.map(project, (global_ids, shapes))
        summed = jax.ops.segment_sum(projected.reshape(-1, NPROJ, ORB).astype(jnp.float32), atom_list, num_segments=ATOMS)
        mixed = jnp.einsum("apq,aqo->apo", coupling, active[:, :, None] * summed, precision=lax.Precision.HIGHEST)
        weighted = (active[:, :, None] * mixed).astype(jnp.bfloat16)
        returned = weighted[atom_list].reshape(devices, CELLS_DEV, ENT_CELL, NPROJ, ORB)

        def accumulate(total, inputs):
            node_ids, matrix_block, shape_block, returned_block = inputs
            local = field[node_ids].astype(jnp.float32)
            result = jnp.einsum("cmn,cno->cmo", matrix_block.astype(jnp.float32), local)
            result = result + jnp.einsum("ckpn,ckpo->cno", shape_block.astype(jnp.float32), returned_block.astype(jnp.float32))
            return total.at[node_ids.reshape(-1)].add(result.reshape(-1, ORB)), None

        start = jnp.zeros((total_rows, ORB), jnp.float32)
        total, _ = lax.scan(accumulate, start, (global_ids, matrices, shapes, returned))
        return total

    first = orbitals.reshape(-1, ORB)
    previous = first.astype(jnp.float32)
    current = operate(first)
    for _ in range(FILTER_DEGREE - 1):
        following = 2.0 * operate(current.astype(jnp.bfloat16)) - previous
        previous, current = current, following
    return current.astype(jnp.bfloat16).reshape(orbitals.shape)
```

```python
import itertools

import jax
import jax.numpy as jnp
from jax import lax
from jax.experimental import pallas as pl
from jax.experimental.pallas import tpu as pltpu
from jax.sharding import PartitionSpec as P

FILTER_DEGREE = 3
STREAMS = 1
GROUP = 8
BF16 = jnp.bfloat16
F32 = jnp.float32


def shifted(x, axes, by):
    sizes = [lax.axis_size(a) for a in axes]
    pairs = []
    for place in itertools.product(*[range(s) for s in sizes]):
        source = 0
        target = 0
        for at, step, size in zip(place, by, sizes):
            source = source * size + at
            target = target * size + (at + step) % size
        pairs.append((source, target))
    return lax.ppermute(x, axes if len(axes) > 1 else axes[0], pairs)


def whole(shape):
    return pl.BlockSpec(shape, lambda c: (0,) * len(shape), pipeline_mode=pl.Buffered(1))


def smem():
    return pl.BlockSpec(memory_space=pltpu.SMEM)


def canonical(places, matrices, shapes):
    cells, nodes = places.shape
    rows = shapes.shape[1]

    def body(place_ref, matrix_ref, shape_ref, joint_ref, straight_ref):
        spots = lax.broadcasted_iota(jnp.int32, (nodes, nodes), 0)
        pick = (spots == place_ref[0]).astype(BF16)
        last = (((1,), (1,)), ((), ()))
        half = jnp.dot(pick, matrix_ref[0], preferred_element_type=F32).astype(BF16)
        joint_ref[0, :, :nodes] = lax.dot_general(
            half, pick, last, preferred_element_type=F32
        ).astype(BF16)
        joint_ref[0, :, nodes:] = lax.dot_general(
            pick, shape_ref[0], last, preferred_element_type=F32
        ).astype(BF16)
        straight_ref[0] = lax.dot_general(
            shape_ref[0], pick, last, preferred_element_type=F32
        ).astype(BF16)

    return pl.pallas_call(
        body,
        grid=(cells,),
        in_specs=[
            pl.BlockSpec((1, 1, nodes), lambda c: (c, 0, 0)),
            pl.BlockSpec((1, nodes, nodes), lambda c: (c, 0, 0)),
            pl.BlockSpec((1, rows, nodes), lambda c: (c, 0, 0)),
        ],
        out_specs=[
            pl.BlockSpec((1, nodes, nodes + rows), lambda c: (c, 0, 0)),
            pl.BlockSpec((1, rows, nodes), lambda c: (c, 0, 0)),
        ],
        out_shape=[
            jax.ShapeDtypeStruct((cells, nodes, nodes + rows), BF16),
            jax.ShapeDtypeStruct((cells, rows, nodes), BF16),
        ],
        name="canonical",
    )(places.reshape(cells, 1, nodes), matrices, shapes)


def project(field, straight, placed, slots, cz, per_atom):
    cells, rows, nodes = straight.shape
    side = field.shape[2]
    deg = side - 1
    breadth = field.shape[3]
    per_cell = rows // per_atom

    def body(placed_ref, field_ref, straight_ref, local_ref, out_ref):
        c = pl.program_id(0)
        u = c // cz * deg
        w = c % cz * deg
        block = field_ref[pl.ds(u, side), pl.ds(w, side)]
        local = block.reshape(nodes, breadth).astype(BF16)
        local_ref[0] = local
        values = jnp.dot(straight_ref[0], local, preferred_element_type=F32).astype(BF16)
        for k in range(per_cell):
            out_ref[placed_ref[c * per_cell + k]] = values[k * per_atom : (k + 1) * per_atom]

    return pl.pallas_call(
        body,
        grid=(cells,),
        in_specs=[
            smem(),
            whole(field.shape),
            pl.BlockSpec((1, rows, nodes), lambda c: (c, 0, 0)),
        ],
        out_specs=[
            pl.BlockSpec((1, nodes, breadth), lambda c: (c, 0, 0)),
            whole((slots, per_atom, breadth)),
        ],
        out_shape=[
            jax.ShapeDtypeStruct((cells, nodes, breadth), BF16),
            jax.ShapeDtypeStruct((slots, per_atom, breadth), BF16),
        ],
        name="project",
    )(placed, field, straight)


def merge(incoming, ids, filled, atoms):
    slots, per_atom, breadth = incoming.shape
    senders = filled.shape[0]
    each = slots // senders

    def body(ids_ref, filled_ref, incoming_ref, sums_ref, sent_ref):
        sums_ref[...] = jnp.zeros_like(sums_ref)
        for g in range(senders):

            def add(j, carry):
                slot = g * each + j
                atom = ids_ref[slot]
                sums_ref[atom] = sums_ref[atom] + incoming_ref[slot].astype(F32)
                return carry

            lax.fori_loop(0, filled_ref[g], add, 0)
        sent_ref[...] = sums_ref[...].astype(BF16)

    return pl.pallas_call(
        body,
        in_specs=[smem(), smem(), pl.BlockSpec(memory_space=pltpu.VMEM)],
        out_specs=[pl.BlockSpec(memory_space=pltpu.VMEM)] * 2,
        out_shape=[
            jax.ShapeDtypeStruct((atoms, per_atom, breadth), F32),
            jax.ShapeDtypeStruct((atoms, per_atom, breadth), BF16),
        ],
        name="merge",
    )(ids, filled, incoming)


def couple(sums, others, high, low, ids, filled, slots):
    atoms, per_atom, breadth = sums.shape
    groups, edge, _ = high.shape
    members = atoms // groups
    senders = filled.shape[0]
    each = slots // senders

    def body(ids_ref, filled_ref, sums_ref, others_ref, high_ref, low_ref, out_ref, kept_ref):
        for g in range(groups):
            part = pl.ds(g * members, members)
            total = sums_ref[part] + others_ref[part].astype(F32)
            total = total.reshape(edge, breadth)
            upper = total.astype(BF16)
            lower = (total - upper.astype(F32)).astype(BF16)
            mixed = jnp.dot(high_ref[g], upper, preferred_element_type=F32)
            mixed = mixed + jnp.dot(low_ref[g], upper, preferred_element_type=F32)
            mixed = mixed + jnp.dot(high_ref[g], lower, preferred_element_type=F32)
            kept_ref[part] = mixed.astype(BF16).reshape(members, per_atom, breadth)
        for g in range(senders):

            def copy(j, carry):
                slot = g * each + j
                out_ref[slot] = kept_ref[ids_ref[slot]]
                return carry

            lax.fori_loop(0, filled_ref[g], copy, 0)

    vmem = pl.BlockSpec(memory_space=pltpu.VMEM)
    return pl.pallas_call(
        body,
        in_specs=[smem(), smem(), vmem, vmem, vmem, vmem],
        out_specs=vmem,
        out_shape=jax.ShapeDtypeStruct((slots, per_atom, breadth), BF16),
        scratch_shapes=[pltpu.VMEM((atoms, per_atom, breadth), BF16)],
        name="couple",
    )(ids, filled, sums, others, high, low)


def apply(joint, local, answers, placed, extended, cz):
    cells, nodes, columns = joint.shape
    slots, per_atom, breadth = answers.shape
    rows = columns - nodes
    per_cell = rows // per_atom
    side = extended[2]
    deg = side - 1

    def body(placed_ref, joint_ref, local_ref, answers_ref, total_ref, stack_ref):
        c = pl.program_id(0)

        @pl.when(c == 0)
        def _():
            total_ref[...] = jnp.zeros_like(total_ref)

        stack_ref[:nodes] = local_ref[0]
        for k in range(per_cell):
            at = nodes + k * per_atom
            stack_ref[at : at + per_atom] = answers_ref[placed_ref[c * per_cell + k]]
        result = jnp.dot(joint_ref[0], stack_ref[...], preferred_element_type=F32)
        u = pl.ds(c // cz * deg, side)
        w = pl.ds(c % cz * deg, side)
        total_ref[u, w] = total_ref[u, w] + result.reshape(side, side, side, breadth)

    shape = extended + (breadth,)
    return pl.pallas_call(
        body,
        grid=(cells,),
        in_specs=[
            smem(),
            pl.BlockSpec((1, nodes, columns), lambda c: (c, 0, 0)),
            pl.BlockSpec((1, nodes, breadth), lambda c: (c, 0, 0)),
            whole(answers.shape),
        ],
        out_specs=whole(shape),
        out_shape=jax.ShapeDtypeStruct(shape, F32),
        scratch_shapes=[pltpu.VMEM((columns, breadth), BF16)],
        name="apply",
    )(placed, joint, local, answers)


def completed(total):
    low_u, high_u = total[:1], total[-1:]
    low_v, high_v = total[:, :, :1], total[:, :, -1:]

    def moved(x, axes, by):
        return shifted(x.astype(BF16), axes, by).astype(F32)

    both = ("gx", "gy")
    from_next_u = moved(low_u, ("gx",), (-1,))
    from_prev_u = moved(high_u, ("gx",), (1,))
    from_next_v = moved(low_v, ("gy",), (-1,))
    from_prev_v = moved(high_v, ("gy",), (1,))
    corner_nn = moved(low_u[:, :, :1], both, (-1, -1))
    corner_np = moved(low_u[:, :, -1:], both, (-1, 1))
    corner_pn = moved(high_u[:, :, :1], both, (1, -1))
    corner_pp = moved(high_u[:, :, -1:], both, (1, 1))
    span_u, _, span_v, _ = total.shape
    rest_v = ((0, 0), (0, 0), (1, span_v - 2), (0, 0))

    def at_ends(first, last, axis):
        shape = list(total.shape)
        shape[axis] = total.shape[axis] - 2
        for other in range(4):
            if other != axis:
                shape[other] = first.shape[other]
        return jnp.concatenate([first, jnp.zeros(shape, F32), last], axis=axis)

    first_row = from_prev_u + at_ends(corner_pp, corner_pn, 2)
    last_row = from_next_u + at_ends(corner_np, corner_nn, 2)
    return total + at_ends(first_row, last_row, 0) + at_ends(from_prev_v, from_next_v, 2)


def on_device(orbitals, cell_matrices, cell_nodes, projectors, entry_atom, coupling, proj_counts):
    span_x, span_y, layers, _ = orbitals.shape
    matrices = cell_matrices[0, 0]
    node_map = cell_nodes[0, 0]
    cells, per_cell, per_atom, nodes = projectors.shape[2:]
    shapes = projectors[0, 0].reshape(cells, per_cell * per_atom, nodes)
    atom_names = entry_atom[0, 0]
    side = round(nodes ** (1 / 3))
    deg = side - 1
    cz = (layers - 1) // deg
    assert span_y == deg and side**3 == nodes and cells * deg == span_x * cz
    entries = cells * per_cell
    n_gx, n_gy = lax.axis_size("gx"), lax.axis_size("gy")
    devices = n_gx * n_gy
    half = n_gy // 2
    senders = devices // 2
    home_atoms = coupling.shape[0]
    atoms = 2 * home_atoms
    each = 2 * max(2, 2 * entries // devices)
    slots = senders * each
    both = ("gx", "gy")
    teams = [
        [p * n_gy + h * half + r for p in range(n_gx) for r in range(half)] for h in range(2)
    ]

    def exchange(x):
        return lax.all_to_all(
            x, both, split_axis=0, concat_axis=0, axis_index_groups=teams, tiled=True
        )

    flat = atom_names.reshape(entries)
    homes = flat // home_atoms
    homes_y = homes % n_gy
    collectors = homes // n_gy * half + homes_y % half
    inner = homes_y // half * home_atoms + flat % home_atoms
    order = jnp.arange(entries, dtype=jnp.int32)
    earlier = (collectors[:, None] == collectors[None, :]) & (order[None, :] < order[:, None])
    placed = collectors * each + jnp.sum(earlier.astype(jnp.int32), axis=1)
    named = placed[None, :] == jnp.arange(slots, dtype=jnp.int32)[:, None]
    sent_ids = jnp.sum(jnp.where(named, inner[None, :] + 1, 0), axis=1) - 1
    ids = exchange(sent_ids.reshape(senders, each))
    filled = jnp.sum((ids >= 0).astype(jnp.int32), axis=1)
    ids = ids.reshape(slots)

    active = (jnp.arange(per_atom, dtype=jnp.int32)[None, :] < proj_counts[:, None]).astype(F32)
    masked = coupling * active[:, :, None] * active[:, None, :]
    partner = shifted(masked, ("gy",), (half,))
    upper_half = lax.axis_index("gy") >= half
    mixers = jnp.where(
        upper_half,
        jnp.concatenate([partner, masked], axis=0),
        jnp.concatenate([masked, partner], axis=0),
    )
    mixers = mixers.reshape(atoms // GROUP, GROUP, per_atom, 1, per_atom)
    own = jnp.eye(GROUP, dtype=F32)[None, :, None, :, None]
    mixers = (mixers * own).reshape(atoms // GROUP, GROUP * per_atom, GROUP * per_atom)
    mix_high = mixers.astype(BF16)
    mix_low = (mixers - mix_high.astype(F32)).astype(BF16)

    cell_ids = jnp.arange(cells, dtype=jnp.int32)[:, None]
    node_w = node_map % layers - cell_ids % cz * deg
    node_v = node_map // layers % (span_y + 1)
    node_u = node_map // (layers * (span_y + 1)) - cell_ids // cz * deg
    places = (node_u * side + node_w) * side + node_v
    joint, straight = canonical(places, matrices, shapes)

    row_next = shifted(orbitals[:1], ("gx",), (-1,))
    column_next = shifted(orbitals[:, :1], ("gy",), (-1,))
    corner_next = shifted(orbitals[:1, :1], both, (-1, -1))
    widened = jnp.concatenate(
        [
            jnp.concatenate([orbitals, column_next], axis=1),
            jnp.concatenate([row_next, corner_next], axis=1),
        ],
        axis=0,
    )
    grid = jnp.transpose(widened, (0, 2, 1, 3)).astype(F32)
    extended = grid.shape[:3]

    def operate(field):
        local, outgoing = project(field, straight, placed, slots, cz, per_atom)
        incoming = exchange(outgoing)
        sums, sent = merge(incoming, ids, filled, atoms)
        others = shifted(sent, ("gy",), (half,))
        replies = couple(sums, others, mix_high, mix_low, ids, filled, slots)
        answers = exchange(replies)
        return completed(apply(joint, local, answers, placed, extended, cz))

    width = grid.shape[3] // STREAMS
    results = []
    for s in range(STREAMS):
        previous = grid[..., s * width : (s + 1) * width]
        current = operate(previous)
        for _ in range(FILTER_DEGREE - 1):
            previous, current = (current, 2.0 * operate(current) - previous)
        results.append(current[:span_x, :, :span_y].astype(BF16))
    filtered = jnp.concatenate(results, axis=-1) if STREAMS > 1 else results[0]
    return jnp.transpose(filtered, (0, 2, 1, 3))


def solution(mesh):
    in_specs = (
        P("gx", "gy", None, None),
        P("gx", "gy", None, None, None),
        P("gx", "gy", None, None),
        P("gx", "gy", None, None, None, None),
        P("gx", "gy", None, None),
        P(("gx", "gy"), None, None),
        P(("gx", "gy")),
    )
    out_specs = P("gx", "gy", None, None)
    return jax.shard_map(
        on_device, mesh=mesh, in_specs=in_specs, out_specs=out_specs, check_vma=False
    )
```

```python
import itertools

import jax
import jax.numpy as jnp
from jax import lax
from jax.experimental import pallas as pl
from jax.experimental.pallas import tpu as pltpu
from jax.sharding import PartitionSpec as P


FILTER_DEGREE = 3
PARTS = 2
GRANT = 20 * 1024 * 1024
GROUP = 8
BF16 = jnp.bfloat16
F32 = jnp.float32


def shifted(x, axes, by):
    sizes = [lax.axis_size(a) for a in axes]
    pairs = []
    for place in itertools.product(*[range(s) for s in sizes]):
        source = 0
        target = 0
        for at, step, size in zip(place, by, sizes):
            source = source * size + at
            target = target * size + (at + step) % size
        pairs.append((source, target))
    return lax.ppermute(x, axes if len(axes) > 1 else axes[0], pairs)


def whole(shape):
    return pl.BlockSpec(shape, lambda c: (0,) * len(shape), pipeline_mode=pl.Buffered(1))


def smem():
    return pl.BlockSpec(memory_space=pltpu.SMEM)


def unread(after):
    return [pl.BlockSpec(memory_space=pl.ANY)] * len(after)


def canonical(places, matrices, shapes):
    cells, nodes = places.shape
    rows = shapes.shape[1]

    def body(place_ref, matrix_ref, shape_ref, stiff_ref, turned_ref, straight_ref):
        spots = lax.broadcasted_iota(jnp.int32, (nodes, nodes), 0)
        pick = (spots == place_ref[0]).astype(BF16)
        last = (((1,), (1,)), ((), ()))
        half = jnp.dot(pick, matrix_ref[0], preferred_element_type=F32).astype(BF16)
        stiff_ref[0] = lax.dot_general(
            half, pick, last, preferred_element_type=F32
        ).astype(BF16)
        turned_ref[0] = lax.dot_general(
            pick, shape_ref[0], last, preferred_element_type=F32
        ).astype(BF16)
        straight_ref[0] = lax.dot_general(
            shape_ref[0], pick, last, preferred_element_type=F32
        ).astype(BF16)

    return pl.pallas_call(
        body,
        grid=(cells,),
        in_specs=[
            pl.BlockSpec((1, 1, nodes), lambda c: (c, 0, 0)),
            pl.BlockSpec((1, nodes, nodes), lambda c: (c, 0, 0)),
            pl.BlockSpec((1, rows, nodes), lambda c: (c, 0, 0)),
        ],
        out_specs=[
            pl.BlockSpec((1, nodes, nodes), lambda c: (c, 0, 0)),
            pl.BlockSpec((1, nodes, rows), lambda c: (c, 0, 0)),
            pl.BlockSpec((1, rows, nodes), lambda c: (c, 0, 0)),
        ],
        out_shape=[
            jax.ShapeDtypeStruct((cells, nodes, nodes), BF16),
            jax.ShapeDtypeStruct((cells, nodes, rows), BF16),
            jax.ShapeDtypeStruct((cells, rows, nodes), BF16),
        ],
        compiler_params=pltpu.CompilerParams(vmem_limit_bytes=GRANT),
        name="canonical",
    )(places.reshape(cells, 1, nodes), matrices, shapes)


def spread(mixers):
    atoms, per_atom, _ = mixers.shape
    groups = atoms // GROUP
    edge = GROUP * per_atom

    def body(mixers_ref, high_ref, low_ref):
        rows = lax.broadcasted_iota(jnp.int32, (edge, edge), 0) // per_atom
        columns = lax.broadcasted_iota(jnp.int32, (edge, edge), 1) // per_atom
        for g in range(groups):
            block = mixers_ref[g * GROUP : (g + 1) * GROUP].reshape(edge, per_atom)
            block = jnp.concatenate([block] * GROUP, axis=1)
            block = jnp.where(rows == columns, block, 0.0)
            high = block.astype(BF16)
            high_ref[g] = high
            low_ref[g] = (block - high.astype(F32)).astype(BF16)

    vmem = pl.BlockSpec(memory_space=pltpu.VMEM)
    return pl.pallas_call(
        body,
        in_specs=[vmem],
        out_specs=[vmem, vmem],
        out_shape=[jax.ShapeDtypeStruct((groups, edge, edge), BF16)] * 2,
        compiler_params=pltpu.CompilerParams(vmem_limit_bytes=GRANT),
        name="spread",
    )(mixers)


def project(field, straight, placed, slots, cz, per_atom):
    cells, rows, nodes = straight.shape
    side = field.shape[2]
    deg = side - 1
    breadth = field.shape[3]
    per_cell = rows // per_atom
    width = breadth // PARTS

    def body(placed_ref, field_ref, straight_ref, local_ref, *out_refs):
        c = pl.program_id(0)
        u = c // cz * deg
        w = c % cz * deg
        block = field_ref[pl.ds(u, side), pl.ds(w, side)]
        local = block.reshape(nodes, breadth).astype(BF16)
        local_ref[0] = local
        values = jnp.dot(straight_ref[0], local, preferred_element_type=F32).astype(BF16)
        for k in range(per_cell):
            slot = placed_ref[c * per_cell + k]
            for s, out_ref in enumerate(out_refs):
                out_ref[slot] = values[
                    k * per_atom : (k + 1) * per_atom, s * width : (s + 1) * width
                ]

    return pl.pallas_call(
        body,
        grid=(cells,),
        in_specs=[
            smem(),
            whole(field.shape),
            pl.BlockSpec((1, rows, nodes), lambda c: (c, 0, 0)),
        ],
        out_specs=[
            pl.BlockSpec((1, nodes, breadth), lambda c: (c, 0, 0)),
        ]
        + [whole((slots, per_atom, width))] * PARTS,
        out_shape=[
            jax.ShapeDtypeStruct((cells, nodes, breadth), BF16),
        ]
        + [jax.ShapeDtypeStruct((slots, per_atom, width), BF16)] * PARTS,
        compiler_params=pltpu.CompilerParams(vmem_limit_bytes=GRANT),
        name="project",
    )(placed, field, straight)


def stiffen(stiff, local, extended, cz):
    cells, nodes, _ = stiff.shape
    breadth = local.shape[2]
    side = extended[2]
    deg = side - 1

    def body(stiff_ref, local_ref, total_ref):
        c = pl.program_id(0)

        @pl.when(c == 0)
        def _():
            total_ref[...] = jnp.zeros_like(total_ref)

        result = jnp.dot(stiff_ref[0], local_ref[0], preferred_element_type=F32)
        u = pl.ds(c // cz * deg, side)
        w = pl.ds(c % cz * deg, side)
        total_ref[u, w] = total_ref[u, w] + result.reshape(side, side, side, breadth)

    shape = extended + (breadth,)
    return pl.pallas_call(
        body,
        grid=(cells,),
        in_specs=[
            pl.BlockSpec((1, nodes, nodes), lambda c: (c, 0, 0)),
            pl.BlockSpec((1, nodes, breadth), lambda c: (c, 0, 0)),
        ],
        out_specs=whole(shape),
        out_shape=jax.ShapeDtypeStruct(shape, F32),
        compiler_params=pltpu.CompilerParams(vmem_limit_bytes=GRANT),
        name="stiffen",
    )(stiff, local)


def merge(incoming, ids, filled, atoms, after):
    slots, per_atom, breadth = incoming.shape
    senders = filled.shape[0]
    each = slots // senders

    def body(ids_ref, filled_ref, incoming_ref, *refs):
        sums_ref, sent_ref = refs[len(after) :]
        sums_ref[...] = jnp.zeros_like(sums_ref)
        for g in range(senders):

            def add(j, carry):
                slot = g * each + j
                atom = ids_ref[slot]
                sums_ref[atom] = sums_ref[atom] + incoming_ref[slot].astype(F32)
                return carry

            lax.fori_loop(0, filled_ref[g], add, 0)
        sent_ref[...] = sums_ref[...].astype(BF16)

    return pl.pallas_call(
        body,
        in_specs=[smem(), smem(), pl.BlockSpec(memory_space=pltpu.VMEM)] + unread(after),
        out_specs=[pl.BlockSpec(memory_space=pltpu.VMEM)] * 2,
        out_shape=[
            jax.ShapeDtypeStruct((atoms, per_atom, breadth), F32),
            jax.ShapeDtypeStruct((atoms, per_atom, breadth), BF16),
        ],
        compiler_params=pltpu.CompilerParams(vmem_limit_bytes=GRANT),
        name="merge",
    )(ids, filled, incoming, *after)


def couple(sums, others, high, low, ids, filled, slots, after):
    atoms, per_atom, breadth = sums.shape
    groups, edge, _ = high.shape
    members = atoms // groups
    senders = filled.shape[0]
    each = slots // senders

    def body(ids_ref, filled_ref, sums_ref, others_ref, high_ref, low_ref, *refs):
        out_ref, kept_ref = refs[len(after) :]
        for g in range(groups):
            part = pl.ds(g * members, members)
            total = sums_ref[part] + others_ref[part].astype(F32)
            total = total.reshape(edge, breadth)
            upper = total.astype(BF16)
            lower = (total - upper.astype(F32)).astype(BF16)
            mixed = jnp.dot(high_ref[g], upper, preferred_element_type=F32)
            mixed = mixed + jnp.dot(low_ref[g], upper, preferred_element_type=F32)
            mixed = mixed + jnp.dot(high_ref[g], lower, preferred_element_type=F32)
            kept_ref[part] = mixed.astype(BF16).reshape(members, per_atom, breadth)
        for g in range(senders):

            def copy(j, carry):
                slot = g * each + j
                out_ref[slot] = kept_ref[ids_ref[slot]]
                return carry

            lax.fori_loop(0, filled_ref[g], copy, 0)

    vmem = pl.BlockSpec(memory_space=pltpu.VMEM)
    return pl.pallas_call(
        body,
        in_specs=[smem(), smem(), vmem, vmem, vmem, vmem] + unread(after),
        out_specs=vmem,
        out_shape=jax.ShapeDtypeStruct((slots, per_atom, breadth), BF16),
        scratch_shapes=[pltpu.VMEM((atoms, per_atom, breadth), BF16)],
        compiler_params=pltpu.CompilerParams(vmem_limit_bytes=GRANT),
        name="couple",
    )(ids, filled, sums, others, high, low, *after)


def apply(turned, answers, begun, placed, part, cz, after):
    cells, nodes, rows = turned.shape
    _, per_atom, breadth = answers.shape
    per_cell = rows // per_atom
    side = begun.shape[2]
    deg = side - 1

    def body(placed_ref, turned_ref, answers_ref, begun_ref, *refs):
        total_ref, stack_ref = refs[len(after) :]
        c = pl.program_id(0)

        @pl.when(c == 0)
        def _():
            total_ref[...] = begun_ref[...]

        for k in range(per_cell):
            at = k * per_atom
            stack_ref[at : at + per_atom] = answers_ref[placed_ref[c * per_cell + k]]
        result = jnp.dot(turned_ref[0], stack_ref[...], preferred_element_type=F32)
        u = pl.ds(c // cz * deg, side)
        w = pl.ds(c % cz * deg, side)
        total_ref[u, w] = total_ref[u, w] + result.reshape(side, side, side, breadth)

    shape = begun.shape[:3] + (breadth,)
    return pl.pallas_call(
        body,
        grid=(cells,),
        in_specs=[
            smem(),
            pl.BlockSpec((1, nodes, rows), lambda c: (c, 0, 0)),
            whole(answers.shape),
            pl.BlockSpec(shape, lambda c: (0, 0, 0, part), pipeline_mode=pl.Buffered(1)),
        ]
        + unread(after),
        out_specs=whole(shape),
        out_shape=jax.ShapeDtypeStruct(shape, F32),
        scratch_shapes=[pltpu.VMEM((rows, breadth), BF16)],
        compiler_params=pltpu.CompilerParams(vmem_limit_bytes=GRANT),
        name="apply",
    )(placed, turned, answers, begun, *after)


def completed(total):
    span_u, span_w, span_v, breadth = total.shape
    low_v = total[:, :, 0].astype(BF16)
    high_v = total[:, :, -1].astype(BF16)
    from_next = shifted(low_v, ("gy",), (-1,)).astype(F32)[:, :, None]
    from_prev = shifted(high_v, ("gy",), (1,)).astype(F32)[:, :, None]
    gap = jnp.zeros((span_u, span_w, span_v - 2, breadth), F32)
    total = total + jnp.concatenate([from_prev, gap, from_next], axis=2)
    low_u = total[0].astype(BF16)
    high_u = total[-1].astype(BF16)
    from_next = shifted(low_u, ("gx",), (-1,)).astype(F32)[None]
    from_prev = shifted(high_u, ("gx",), (1,)).astype(F32)[None]
    gap = jnp.zeros((span_u - 2, span_w, span_v, breadth), F32)
    return total + jnp.concatenate([from_prev, gap, from_next], axis=0)


def on_device(orbitals, cell_matrices, cell_nodes, projectors, entry_atom, coupling, proj_counts):
    span_x, span_y, layers, _ = orbitals.shape
    matrices = cell_matrices[0, 0]
    node_map = cell_nodes[0, 0]
    cells, per_cell, per_atom, nodes = projectors.shape[2:]
    shapes = projectors[0, 0].reshape(cells, per_cell * per_atom, nodes)
    atom_names = entry_atom[0, 0]
    side = round(nodes ** (1 / 3))
    deg = side - 1
    cz = (layers - 1) // deg
    assert span_y == deg and side**3 == nodes and cells * deg == span_x * cz
    entries = cells * per_cell
    n_gx, n_gy = lax.axis_size("gx"), lax.axis_size("gy")
    devices = n_gx * n_gy
    half = n_gy // 2
    senders = devices // 2
    home_atoms = coupling.shape[0]
    atoms = 2 * home_atoms
    each = 2 * max(2, 2 * entries // devices)
    slots = senders * each
    both = ("gx", "gy")
    teams = [
        [p * n_gy + h * half + r for p in range(n_gx) for r in range(half)] for h in range(2)
    ]

    def exchange(x):
        return lax.all_to_all(
            x, both, split_axis=0, concat_axis=0, axis_index_groups=teams, tiled=True
        )

    flat = atom_names.reshape(entries)
    homes = flat // home_atoms
    homes_y = homes % n_gy
    collectors = homes // n_gy * half + homes_y % half
    inner = homes_y // half * home_atoms + flat % home_atoms
    order = jnp.arange(entries, dtype=jnp.int32)
    earlier = (collectors[:, None] == collectors[None, :]) & (order[None, :] < order[:, None])
    placed = collectors * each + jnp.sum(earlier.astype(jnp.int32), axis=1)
    named = placed[None, :] == jnp.arange(slots, dtype=jnp.int32)[:, None]
    sent_ids = jnp.sum(jnp.where(named, inner[None, :] + 1, 0), axis=1) - 1
    ids = exchange(sent_ids.reshape(senders, each))
    filled = jnp.sum((ids >= 0).astype(jnp.int32), axis=1)
    ids = ids.reshape(slots)

    active = (jnp.arange(per_atom, dtype=jnp.int32)[None, :] < proj_counts[:, None]).astype(F32)
    masked = coupling * active[:, :, None] * active[:, None, :]
    partner = shifted(masked.reshape(-1, 128), ("gy",), (half,)).reshape(coupling.shape)
    upper_half = lax.axis_index("gy") >= half
    mixers = jnp.where(
        upper_half,
        jnp.concatenate([partner, masked], axis=0),
        jnp.concatenate([masked, partner], axis=0),
    )
    mix_high, mix_low = spread(mixers)

    cell_ids = jnp.arange(cells, dtype=jnp.int32)[:, None]
    node_w = node_map % layers - cell_ids % cz * deg
    node_v = node_map // layers % (span_y + 1)
    node_u = node_map // (layers * (span_y + 1)) - cell_ids // cz * deg
    places = (node_u * side + node_w) * side + node_v
    stiff, turned, straight = canonical(places, matrices, shapes)

    row_next = shifted(orbitals[:1], ("gx",), (-1,))
    column_next = shifted(orbitals[:, :1], ("gy",), (-1,))
    corner_next = shifted(orbitals[:1, :1], both, (-1, -1))
    widened = jnp.concatenate(
        [
            jnp.concatenate([orbitals, column_next], axis=1),
            jnp.concatenate([row_next, corner_next], axis=1),
        ],
        axis=0,
    )
    grid = jnp.transpose(widened, (0, 2, 1, 3)).astype(F32)
    extended = grid.shape[:3]

    def advance(field, older):
        local, *outgoing = project(field, straight, placed, slots, cz, per_atom)
        image = stiffen(stiff, local, extended, cz)
        after = (image,)
        gathered = []
        for packet in outgoing:
            incoming = exchange(packet)
            gathered.append(merge(incoming, ids, filled, atoms, after))
            after = (gathered[-1][0],)
        answers = []
        for sums, sent in gathered:
            others = shifted(sent, ("gy",), (half,))
            replies = couple(sums, others, mix_high, mix_low, ids, filled, slots, after)
            answers.append(exchange(replies))
            after = (replies,)
        totals = []
        for part in range(PARTS):
            totals.append(apply(turned, answers[part], image, placed, part, cz, after))
            after = (totals[-1],)
        image = completed(jnp.concatenate(totals, axis=-1))
        return image if older is None else 2.0 * image - older

    older, field = None, grid
    for _ in range(FILTER_DEGREE):
        older, field = field, advance(field, older)
    filtered = field[:span_x, :, :span_y].astype(BF16)
    return jnp.transpose(filtered, (0, 2, 1, 3))


def solution(mesh):
    in_specs = (
        P("gx", "gy", None, None),
        P("gx", "gy", None, None, None),
        P("gx", "gy", None, None),
        P("gx", "gy", None, None, None, None),
        P("gx", "gy", None, None),
        P(("gx", "gy"), None, None),
        P(("gx", "gy")),
    )
    out_specs = P("gx", "gy", None, None)
    return jax.shard_map(
        on_device, mesh=mesh, in_specs=in_specs, out_specs=out_specs, check_vma=False
    )
```

```python
import itertools

import jax
import jax.numpy as jnp
from jax import lax
from jax.experimental import pallas as pl
from jax.experimental.pallas import tpu as pltpu
from jax.sharding import PartitionSpec as P


FILTER_DEGREE = 3
PARTS = 1
UNIT = 8
TIGHT = 54
NARROW = 188
MODE = "cond"
GRANT = 20 * 1024 * 1024
GROUP = 8
BF16 = jnp.bfloat16
F32 = jnp.float32


def shifted(x, axes, by):
    sizes = [lax.axis_size(a) for a in axes]
    pairs = []
    for place in itertools.product(*[range(s) for s in sizes]):
        source = 0
        target = 0
        for at, step, size in zip(place, by, sizes):
            source = source * size + at
            target = target * size + (at + step) % size
        pairs.append((source, target))
    return lax.ppermute(x, axes if len(axes) > 1 else axes[0], pairs)


def whole(shape):
    return pl.BlockSpec(shape, lambda c: (0,) * len(shape), pipeline_mode=pl.Buffered(1))


def smem():
    return pl.BlockSpec(memory_space=pltpu.SMEM)


def unread(after):
    return [pl.BlockSpec(memory_space=pl.ANY)] * len(after)


def canonical(places, matrices, shapes):
    cells, nodes = places.shape
    rows = shapes.shape[1]

    def body(place_ref, matrix_ref, shape_ref, stiff_ref, turned_ref, straight_ref):
        spots = lax.broadcasted_iota(jnp.int32, (nodes, nodes), 0)
        pick = (spots == place_ref[0]).astype(BF16)
        last = (((1,), (1,)), ((), ()))
        half = jnp.dot(pick, matrix_ref[0], preferred_element_type=F32).astype(BF16)
        stiff_ref[0] = lax.dot_general(
            half, pick, last, preferred_element_type=F32
        ).astype(BF16)
        turned_ref[0] = lax.dot_general(
            pick, shape_ref[0], last, preferred_element_type=F32
        ).astype(BF16)
        straight_ref[0] = lax.dot_general(
            shape_ref[0], pick, last, preferred_element_type=F32
        ).astype(BF16)

    return pl.pallas_call(
        body,
        grid=(cells,),
        in_specs=[
            pl.BlockSpec((1, 1, nodes), lambda c: (c, 0, 0)),
            pl.BlockSpec((1, nodes, nodes), lambda c: (c, 0, 0)),
            pl.BlockSpec((1, rows, nodes), lambda c: (c, 0, 0)),
        ],
        out_specs=[
            pl.BlockSpec((1, nodes, nodes), lambda c: (c, 0, 0)),
            pl.BlockSpec((1, nodes, rows), lambda c: (c, 0, 0)),
            pl.BlockSpec((1, rows, nodes), lambda c: (c, 0, 0)),
        ],
        out_shape=[
            jax.ShapeDtypeStruct((cells, nodes, nodes), BF16),
            jax.ShapeDtypeStruct((cells, nodes, rows), BF16),
            jax.ShapeDtypeStruct((cells, rows, nodes), BF16),
        ],
        compiler_params=pltpu.CompilerParams(vmem_limit_bytes=GRANT),
        name="canonical",
    )(places.reshape(cells, 1, nodes), matrices, shapes)


def spread(mixers):
    atoms, per_atom, _ = mixers.shape
    groups = atoms // GROUP
    edge = GROUP * per_atom

    def body(mixers_ref, high_ref, low_ref):
        rows = lax.broadcasted_iota(jnp.int32, (edge, edge), 0) // per_atom
        columns = lax.broadcasted_iota(jnp.int32, (edge, edge), 1) // per_atom
        for g in range(groups):
            block = mixers_ref[g * GROUP : (g + 1) * GROUP].reshape(edge, per_atom)
            block = jnp.concatenate([block] * GROUP, axis=1)
            block = jnp.where(rows == columns, block, 0.0)
            high = block.astype(BF16)
            high_ref[g] = high
            low_ref[g] = (block - high.astype(F32)).astype(BF16)

    vmem = pl.BlockSpec(memory_space=pltpu.VMEM)
    return pl.pallas_call(
        body,
        in_specs=[vmem],
        out_specs=[vmem, vmem],
        out_shape=[jax.ShapeDtypeStruct((groups, edge, edge), BF16)] * 2,
        compiler_params=pltpu.CompilerParams(vmem_limit_bytes=GRANT),
        name="spread",
    )(mixers)


def project(field, straight, starts, room, cz, per_atom):
    cells, rows, nodes = straight.shape
    side = field.shape[2]
    deg = side - 1
    breadth = field.shape[3]
    per_cell = rows // per_atom
    width = breadth // PARTS
    units = per_atom // UNIT

    def body(starts_ref, field_ref, straight_ref, local_ref, *out_refs):
        c = pl.program_id(0)
        u = c // cz * deg
        w = c % cz * deg
        block = field_ref[pl.ds(u, side), pl.ds(w, side)]
        local = block.reshape(nodes, breadth).astype(BF16)
        local_ref[0] = local
        values = jnp.dot(straight_ref[0], local, preferred_element_type=F32)
        for k in range(per_cell):
            start = starts_ref[c * per_cell + k]
            for s, out_ref in enumerate(out_refs):
                piece = values[k * per_atom : (k + 1) * per_atom, s * width : (s + 1) * width]
                out_ref[pl.ds(start, units)] = piece.reshape(units, UNIT, width).astype(BF16)

    return pl.pallas_call(
        body,
        grid=(cells,),
        in_specs=[
            smem(),
            whole(field.shape),
            pl.BlockSpec((1, rows, nodes), lambda c: (c, 0, 0)),
        ],
        out_specs=[
            pl.BlockSpec((1, nodes, breadth), lambda c: (c, 0, 0)),
        ]
        + [whole((room, UNIT, width))] * PARTS,
        out_shape=[
            jax.ShapeDtypeStruct((cells, nodes, breadth), BF16),
        ]
        + [jax.ShapeDtypeStruct((room, UNIT, width), BF16)] * PARTS,
        compiler_params=pltpu.CompilerParams(vmem_limit_bytes=GRANT),
        name="project",
    )(starts, field, straight)


def stiffen(stiff, local, extended, cz):
    cells, nodes, _ = stiff.shape
    breadth = local.shape[2]
    side = extended[2]
    deg = side - 1

    def body(stiff_ref, local_ref, total_ref):
        c = pl.program_id(0)

        @pl.when(c == 0)
        def _():
            total_ref[...] = jnp.zeros_like(total_ref)

        result = jnp.dot(stiff_ref[0], local_ref[0], preferred_element_type=F32)
        u = pl.ds(c // cz * deg, side)
        w = pl.ds(c % cz * deg, side)
        total_ref[u, w] = total_ref[u, w] + result.reshape(side, side, side, breadth)

    shape = extended + (breadth,)
    return pl.pallas_call(
        body,
        grid=(cells,),
        in_specs=[
            pl.BlockSpec((1, nodes, nodes), lambda c: (c, 0, 0)),
            pl.BlockSpec((1, nodes, breadth), lambda c: (c, 0, 0)),
        ],
        out_specs=whole(shape),
        out_shape=jax.ShapeDtypeStruct(shape, F32),
        compiler_params=pltpu.CompilerParams(vmem_limit_bytes=GRANT),
        name="stiffen",
    )(stiff, local)


def merge(incoming, tables, atoms, units, span, after):
    breadth = incoming.shape[2]
    ids, begins, filled, spots, _ = tables
    senders = filled.shape[0]
    each = ids.shape[0] // senders

    def body(ids_ref, begins_ref, filled_ref, spots_ref, incoming_ref, *refs):
        sums_ref, sent_ref = refs[len(after) :]
        sums_ref[...] = jnp.zeros_like(sums_ref)

        def sender(g, carry):
            def add(j, carry):
                slot = g * each + j
                into = pl.ds(ids_ref[slot] * units, units)
                piece = incoming_ref[pl.ds(begins_ref[slot], units)].astype(F32)
                sums_ref[into] = sums_ref[into] + piece
                return carry

            return lax.fori_loop(0, filled_ref[g], add, carry)

        lax.fori_loop(0, senders, sender, 0)

        def pack(a, carry):
            piece = sums_ref[pl.ds(a * units, units)]
            sent_ref[pl.ds(spots_ref[a], units)] = piece.astype(BF16)
            return carry

        lax.fori_loop(0, atoms, pack, 0, unroll=4)

    return pl.pallas_call(
        body,
        in_specs=[smem()] * 4 + [pl.BlockSpec(memory_space=pltpu.VMEM)] + unread(after),
        out_specs=[pl.BlockSpec(memory_space=pltpu.VMEM)] * 2,
        out_shape=[
            jax.ShapeDtypeStruct((atoms * units, UNIT, breadth), F32),
            jax.ShapeDtypeStruct((span, UNIT, breadth), BF16),
        ],
        compiler_params=pltpu.CompilerParams(vmem_limit_bytes=GRANT),
        name="merge",
    )(ids, begins, filled, spots, incoming, *after)


def couple(sums, others, high, low, tables, units, room, after):
    breadth = sums.shape[2]
    groups, edge, _ = high.shape
    ids, begins, filled, spots, shared = tables
    senders = filled.shape[0]
    each = ids.shape[0] // senders
    rows = units * UNIT

    def body(ids_ref, begins_ref, filled_ref, spots_ref, shared_ref, sums_ref, others_ref, *refs):
        high_ref, low_ref = refs[:2]
        out_ref, total_ref, kept_ref = refs[2 + len(after) :]

        def mix(g, carry):
            for m in range(GROUP):
                a = g * GROUP + m
                piece = others_ref[pl.ds(spots_ref[a], units)].astype(F32)
                piece = jnp.where(shared_ref[a] > 0, piece, 0.0)
                piece = sums_ref[pl.ds(a * units, units)] + piece
                total_ref[m * rows : (m + 1) * rows] = piece.reshape(rows, breadth)
            total = total_ref[...]
            upper = total.astype(BF16)
            lower = (total - upper.astype(F32)).astype(BF16)
            mixed = jnp.dot(high_ref[g], upper, preferred_element_type=F32)
            mixed = mixed + jnp.dot(low_ref[g], upper, preferred_element_type=F32)
            mixed = mixed + jnp.dot(high_ref[g], lower, preferred_element_type=F32)
            mixed = mixed.reshape(GROUP * units, UNIT, breadth).astype(BF16)
            kept_ref[pl.ds(g * GROUP * units, GROUP * units)] = mixed
            return carry

        lax.fori_loop(0, groups, mix, 0, unroll=2)

        def sender(g, carry):
            def copy(j, carry):
                slot = g * each + j
                piece = kept_ref[pl.ds(ids_ref[slot] * units, units)]
                out_ref[pl.ds(begins_ref[slot], units)] = piece
                return carry

            return lax.fori_loop(0, filled_ref[g], copy, carry)

        lax.fori_loop(0, senders, sender, 0)

    vmem = pl.BlockSpec(memory_space=pltpu.VMEM)
    return pl.pallas_call(
        body,
        in_specs=[smem()] * 5 + [vmem] * 4 + unread(after),
        out_specs=vmem,
        out_shape=jax.ShapeDtypeStruct((room, UNIT, breadth), BF16),
        scratch_shapes=[
            pltpu.VMEM((edge, breadth), F32),
            pltpu.VMEM((sums.shape[0], UNIT, breadth), BF16),
        ],
        compiler_params=pltpu.CompilerParams(vmem_limit_bytes=GRANT),
        name="couple",
    )(ids, begins, filled, spots, shared, sums, others, high, low, *after)


def apply(turned, answers, begun, starts, used, part, cz, per_atom, after):
    cells, nodes, rows = turned.shape
    breadth = answers.shape[2]
    per_cell = rows // per_atom
    units = per_atom // UNIT
    side = begun.shape[2]
    deg = side - 1

    def body(starts_ref, used_ref, turned_ref, answers_ref, begun_ref, *refs):
        total_ref, stack_ref = refs[len(after) :]
        c = pl.program_id(0)

        @pl.when(c == 0)
        def _():
            total_ref[...] = begun_ref[...]

        row = lax.broadcasted_iota(jnp.int32, (per_atom, breadth), 0)
        for k in range(per_cell):
            entry = c * per_cell + k
            piece = answers_ref[pl.ds(starts_ref[entry], units)].astype(F32)
            piece = piece.reshape(per_atom, breadth)
            piece = jnp.where(row < used_ref[entry] * UNIT, piece, 0.0)
            stack_ref[k * per_atom : (k + 1) * per_atom] = piece.astype(BF16)
        result = jnp.dot(turned_ref[0], stack_ref[...], preferred_element_type=F32)
        u = pl.ds(c // cz * deg, side)
        w = pl.ds(c % cz * deg, side)
        total_ref[u, w] = total_ref[u, w] + result.reshape(side, side, side, breadth)

    shape = begun.shape[:3] + (breadth,)
    return pl.pallas_call(
        body,
        grid=(cells,),
        in_specs=[
            smem(),
            smem(),
            pl.BlockSpec((1, nodes, rows), lambda c: (c, 0, 0)),
            whole(answers.shape),
            pl.BlockSpec(shape, lambda c: (0, 0, 0, part), pipeline_mode=pl.Buffered(1)),
        ]
        + unread(after),
        out_specs=whole(shape),
        out_shape=jax.ShapeDtypeStruct(shape, F32),
        scratch_shapes=[pltpu.VMEM((rows, breadth), BF16)],
        compiler_params=pltpu.CompilerParams(vmem_limit_bytes=GRANT),
        name="apply",
    )(starts, used, turned, answers, begun, *after)


def completed(total):
    span_u, span_w, span_v, breadth = total.shape
    low_v = total[:, :, 0].astype(BF16)
    high_v = total[:, :, -1].astype(BF16)
    from_next = shifted(low_v, ("gy",), (-1,)).astype(F32)[:, :, None]
    from_prev = shifted(high_v, ("gy",), (1,)).astype(F32)[:, :, None]
    gap = jnp.zeros((span_u, span_w, span_v - 2, breadth), F32)
    total = total + jnp.concatenate([from_prev, gap, from_next], axis=2)
    low_u = total[0].astype(BF16)
    high_u = total[-1].astype(BF16)
    from_next = shifted(low_u, ("gx",), (-1,)).astype(F32)[None]
    from_prev = shifted(high_u, ("gx",), (1,)).astype(F32)[None]
    gap = jnp.zeros((span_u - 2, span_w, span_v, breadth), F32)
    return total + jnp.concatenate([from_prev, gap, from_next], axis=0)


def on_device(orbitals, cell_matrices, cell_nodes, projectors, entry_atom, coupling, proj_counts):
    span_x, span_y, layers, _ = orbitals.shape
    matrices = cell_matrices[0, 0]
    node_map = cell_nodes[0, 0]
    cells, per_cell, per_atom, nodes = projectors.shape[2:]
    shapes = projectors[0, 0].reshape(cells, per_cell * per_atom, nodes)
    atom_names = entry_atom[0, 0]
    side = round(nodes ** (1 / 3))
    deg = side - 1
    cz = (layers - 1) // deg
    assert span_y == deg and side**3 == nodes and cells * deg == span_x * cz
    entries = cells * per_cell
    n_gx, n_gy = lax.axis_size("gx"), lax.axis_size("gy")
    devices = n_gx * n_gy
    half = n_gy // 2
    senders = devices // 2
    home_atoms = coupling.shape[0]
    atoms = 2 * home_atoms
    each = 2 * max(2, 2 * entries // devices)
    slots = senders * each
    both = ("gx", "gy")
    teams = [
        [p * n_gy + h * half + r for p in range(n_gx) for r in range(half)] for h in range(2)
    ]

    def exchange(x):
        return lax.all_to_all(
            x, both, split_axis=0, concat_axis=0, axis_index_groups=teams, tiled=True
        )

    units = per_atom // UNIT
    my_x, my_y = lax.axis_index("gx"), lax.axis_index("gy")
    my_half, my_place = my_y // half, my_y % half
    me = my_x * n_gy + my_y
    mine = my_x * half + my_place

    notes = jnp.concatenate([atom_names.reshape(entries), proj_counts])
    notes = jnp.broadcast_to(notes, (devices, entries + home_atoms))
    notes = lax.all_to_all(notes, both, split_axis=0, concat_axis=0, tiled=True)
    names, counts = notes[:, :entries], notes[:, entries:]
    needs = (counts + UNIT - 1) // UNIT
    homes, inner = names // home_atoms, names % home_atoms
    homes_y = homes % n_gy
    at_home = (homes[:, :, None] == jnp.arange(devices)).astype(BF16)
    at_inner = (inner[:, :, None] == jnp.arange(home_atoms)).astype(BF16)
    picked = jnp.einsum("seh,hi->sei", at_home, needs.astype(BF16), preferred_element_type=F32)
    sizes = jnp.sum(picked * at_inner.astype(F32), axis=2).astype(jnp.int32)
    collectors = homes // n_gy * half + homes_y % half
    held = homes_y // half * home_atoms + inner

    def by_half(x):
        return x.reshape((n_gx, 2, half) + x.shape[1:])

    split = [
        jnp.einsum(
            "seh,sei->hi",
            by_half(at_home)[:, h].reshape((senders,) + at_home.shape[1:]),
            by_half(at_inner)[:, h].reshape((senders,) + at_inner.shape[1:]),
            preferred_element_type=F32,
        )
        for h in range(2)
    ]
    common = ((split[0] > 0) & (split[1] > 0)).astype(jnp.int32)
    at_collector = collectors[:, :, None] == jnp.arange(senders)
    loads = jnp.sum(jnp.where(at_collector, sizes[:, :, None], 0), axis=1)
    crossing = jnp.sum(by_half(common * needs), axis=(1, 3))
    fits = (jnp.max(loads) + units - 1 <= TIGHT * each * units // 64) & (
        jnp.max(crossing) + units <= NARROW * atoms * units // 256
    )

    def of_me(x):
        return lax.dynamic_index_in_dim(x, me, 0, keepdims=False)

    def of_my_half(x):
        x = lax.dynamic_index_in_dim(by_half(x), my_half, 1, keepdims=False)
        return x.reshape((senders,) + x.shape[2:])

    def hosted(x):
        x = lax.dynamic_index_in_dim(by_half(x), my_x, 0, keepdims=False)
        return lax.dynamic_index_in_dim(x, my_place, 1, keepdims=False).reshape(atoms)

    before = jnp.arange(entries)[:, None] < jnp.arange(entries)[None, :]
    own, used = of_me(collectors), of_me(sizes)
    ahead = before & (own[:, None] == own[None, :])
    offsets = jnp.sum(jnp.where(ahead, used[:, None], 0), axis=0)
    theirs = (of_my_half(collectors) == mine).astype(BF16)
    earlier = before.astype(BF16)
    ranks = jnp.dot(theirs, earlier, preferred_element_type=F32).astype(jnp.int32)
    lengths = theirs * of_my_half(sizes).astype(BF16)
    shifts = jnp.dot(lengths, earlier, preferred_element_type=F32).astype(jnp.int32)
    chosen = (ranks[:, None, :] == jnp.arange(each)[:, None]) & (theirs[:, None, :] > 0)
    ids = jnp.sum(jnp.where(chosen, of_my_half(held)[:, None, :], 0), axis=2).reshape(slots)
    places_in = jnp.sum(jnp.where(chosen, shifts[:, None, :], 0), axis=2)
    filled = jnp.sum(theirs.astype(F32), axis=1).astype(jnp.int32)
    shared = hosted(common)
    moved = shared * hosted(needs)
    upto = jnp.arange(atoms)[:, None] < jnp.arange(atoms)[None, :]
    spots = jnp.sum(jnp.where(upto, moved[:, None], 0), axis=0)

    partner = shifted(coupling.reshape(-1, 128), ("gy",), (half,)).reshape(coupling.shape)
    mixers = jnp.where(
        my_half > 0,
        jnp.concatenate([partner, coupling], axis=0),
        jnp.concatenate([coupling, partner], axis=0),
    )
    active = (jnp.arange(per_atom)[None, :] < hosted(counts)[:, None]).astype(F32)
    mixers = mixers * active[:, :, None] * active[:, None, :]
    mix_high, mix_low = spread(mixers)

    cell_ids = jnp.arange(cells, dtype=jnp.int32)[:, None]
    node_w = node_map % layers - cell_ids % cz * deg
    node_v = node_map // layers % (span_y + 1)
    node_u = node_map // (layers * (span_y + 1)) - cell_ids // cz * deg
    places = (node_u * side + node_w) * side + node_v
    stiff, turned, straight = canonical(places, matrices, shapes)

    row_next = shifted(orbitals[:1], ("gx",), (-1,))
    column_next = shifted(orbitals[:, :1], ("gy",), (-1,))
    corner_next = shifted(orbitals[:1, :1], both, (-1, -1))
    widened = jnp.concatenate(
        [
            jnp.concatenate([orbitals, column_next], axis=1),
            jnp.concatenate([row_next, corner_next], axis=1),
        ],
        axis=0,
    )
    grid = jnp.transpose(widened, (0, 2, 1, 3)).astype(F32)
    extended = grid.shape[:3]

    def advance(field, older, cap, span):
        room = senders * cap
        starts = own * cap + offsets
        begins = (places_in + jnp.arange(senders)[:, None] * cap).reshape(slots)
        tables = (ids, begins, filled, spots, shared)
        local, *outgoing = project(field, straight, starts, room, cz, per_atom)
        image = stiffen(stiff, local, extended, cz)
        after = (image,)
        gathered = []
        for packet in outgoing:
            incoming = exchange(packet)
            gathered.append(merge(incoming, tables, atoms, units, span, after))
            after = (gathered[-1][0],)
        answers = []
        for sums, sent in gathered:
            others = shifted(sent, ("gy",), (half,))
            replies = couple(
                sums, others, mix_high, mix_low, tables, units, room, after
            )
            answers.append(exchange(replies))
            after = (replies,)
        totals = []
        for part in range(PARTS):
            totals.append(
                apply(turned, answers[part], image, starts, used, part, cz, per_atom, after)
            )
            after = (totals[-1],)
        image = completed(jnp.concatenate(totals, axis=-1) if PARTS > 1 else totals[0])
        return image if older is None else 2.0 * image - older

    def packed():
        cap = TIGHT * each * units // 64
        span = NARROW * atoms * units // 256
        older, field = None, grid
        for _ in range(FILTER_DEGREE):
            older, field = field, advance(field, older, cap, span)
        return field[:span_x, :, :span_y].astype(BF16)

    def roomy():
        cap = (each + 1) * units
        span = (atoms + 1) * units

        def step(at, fields):
            older, field = fields
            image = advance(field, None, cap, span)
            return field, jnp.where(at == 0, image, 2.0 * image - older)

        fields = (jnp.zeros_like(grid), grid)
        field = lax.fori_loop(0, FILTER_DEGREE, step, fields)[1]
        return field[:span_x, :, :span_y].astype(BF16)

    if MODE == "cond":
        filtered = lax.cond(fits, packed, roomy)
    else:
        filtered = packed() if MODE == "fast" else roomy()
    return jnp.transpose(filtered, (0, 2, 1, 3))


def solution(mesh):
    in_specs = (
        P("gx", "gy", None, None),
        P("gx", "gy", None, None, None),
        P("gx", "gy", None, None),
        P("gx", "gy", None, None, None, None),
        P("gx", "gy", None, None),
        P(("gx", "gy"), None, None),
        P(("gx", "gy")),
    )
    out_specs = P("gx", "gy", None, None)
    return jax.shard_map(
        on_device, mesh=mesh, in_specs=in_specs, out_specs=out_specs, check_vma=False
    )
```

```python
import itertools

import jax
import jax.numpy as jnp
import numpy as np
from jax import lax
from jax.experimental import pallas as pl
from jax.experimental.pallas import tpu as pltpu
from jax.sharding import PartitionSpec as P


FILTER_DEGREE = 3
PARTS = 1
UNIT = 8
TIGHT = 47
NARROW = 172
TURNS = 4
MODE = "cond"
GRANT = 20 * 1024 * 1024
GROUP = 8
BF16 = jnp.bfloat16
F32 = jnp.float32


def shifted(x, axes, by):
    sizes = [lax.axis_size(a) for a in axes]
    pairs = []
    for place in itertools.product(*[range(s) for s in sizes]):
        source = 0
        target = 0
        for at, step, size in zip(place, by, sizes):
            source = source * size + at
            target = target * size + (at + step) % size
        pairs.append((source, target))
    return lax.ppermute(x, axes if len(axes) > 1 else axes[0], pairs)


def whole(shape):
    return pl.BlockSpec(shape, lambda c: (0,) * len(shape), pipeline_mode=pl.Buffered(1))


def smem():
    return pl.BlockSpec(memory_space=pltpu.SMEM)


def unread(after):
    return [pl.BlockSpec(memory_space=pl.ANY)] * len(after)


def canonical(places, matrices, shapes):
    cells, nodes = places.shape
    rows = shapes.shape[1]

    def body(place_ref, matrix_ref, shape_ref, stiff_ref, turned_ref, straight_ref):
        spots = lax.broadcasted_iota(jnp.int32, (nodes, nodes), 0)
        pick = (spots == place_ref[0]).astype(BF16)
        last = (((1,), (1,)), ((), ()))
        half = jnp.dot(pick, matrix_ref[0], preferred_element_type=F32).astype(BF16)
        stiff_ref[0] = lax.dot_general(
            half, pick, last, preferred_element_type=F32
        ).astype(BF16)
        turned_ref[0] = lax.dot_general(
            pick, shape_ref[0], last, preferred_element_type=F32
        ).astype(BF16)
        straight_ref[0] = lax.dot_general(
            shape_ref[0], pick, last, preferred_element_type=F32
        ).astype(BF16)

    return pl.pallas_call(
        body,
        grid=(cells,),
        in_specs=[
            pl.BlockSpec((1, 1, nodes), lambda c: (c, 0, 0)),
            pl.BlockSpec((1, nodes, nodes), lambda c: (c, 0, 0)),
            pl.BlockSpec((1, rows, nodes), lambda c: (c, 0, 0)),
        ],
        out_specs=[
            pl.BlockSpec((1, nodes, nodes), lambda c: (c, 0, 0)),
            pl.BlockSpec((1, nodes, rows), lambda c: (c, 0, 0)),
            pl.BlockSpec((1, rows, nodes), lambda c: (c, 0, 0)),
        ],
        out_shape=[
            jax.ShapeDtypeStruct((cells, nodes, nodes), BF16),
            jax.ShapeDtypeStruct((cells, nodes, rows), BF16),
            jax.ShapeDtypeStruct((cells, rows, nodes), BF16),
        ],
        compiler_params=pltpu.CompilerParams(vmem_limit_bytes=GRANT),
        name="canonical",
    )(places.reshape(cells, 1, nodes), matrices, shapes)


def spread(mixers, after):
    atoms, per_atom, _ = mixers.shape
    groups = atoms // GROUP
    edge = GROUP * per_atom

    def body(mixers_ref, *refs):
        high_ref, low_ref = refs[len(after) :]
        rows = lax.broadcasted_iota(jnp.int32, (edge, edge), 0) // per_atom
        columns = lax.broadcasted_iota(jnp.int32, (edge, edge), 1) // per_atom
        for g in range(groups):
            block = mixers_ref[g * GROUP : (g + 1) * GROUP].reshape(edge, per_atom)
            block = jnp.concatenate([block] * GROUP, axis=1)
            block = jnp.where(rows == columns, block, 0.0)
            high = block.astype(BF16)
            high_ref[g] = high
            low_ref[g] = (block - high.astype(F32)).astype(BF16)

    vmem = pl.BlockSpec(memory_space=pltpu.VMEM)
    return pl.pallas_call(
        body,
        in_specs=[vmem] + unread(after),
        out_specs=[vmem, vmem],
        out_shape=[jax.ShapeDtypeStruct((groups, edge, edge), BF16)] * 2,
        compiler_params=pltpu.CompilerParams(vmem_limit_bytes=GRANT),
        name="spread",
    )(mixers, *after)


def project(field, straight, starts, room, cz, per_atom):
    cells, rows, nodes = straight.shape
    side = field.shape[2]
    deg = side - 1
    breadth = field.shape[3]
    per_cell = rows // per_atom
    width = breadth // PARTS
    units = per_atom // UNIT

    def body(starts_ref, field_ref, straight_ref, local_ref, *out_refs):
        c = pl.program_id(0)
        u = c // cz * deg
        w = c % cz * deg
        block = field_ref[pl.ds(u, side), pl.ds(w, side)]
        local = block.reshape(nodes, breadth).astype(BF16)
        local_ref[0] = local
        values = jnp.dot(straight_ref[0], local, preferred_element_type=F32)
        for k in range(per_cell):
            start = starts_ref[c * per_cell + k]
            for s, out_ref in enumerate(out_refs):
                piece = values[k * per_atom : (k + 1) * per_atom, s * width : (s + 1) * width]
                out_ref[pl.ds(start, units)] = piece.reshape(units, UNIT, width).astype(BF16)

    return pl.pallas_call(
        body,
        grid=(cells,),
        in_specs=[
            smem(),
            whole(field.shape),
            pl.BlockSpec((1, rows, nodes), lambda c: (c, 0, 0)),
        ],
        out_specs=[
            pl.BlockSpec((1, nodes, breadth), lambda c: (c, 0, 0)),
        ]
        + [whole((room, UNIT, width))] * PARTS,
        out_shape=[
            jax.ShapeDtypeStruct((cells, nodes, breadth), BF16),
        ]
        + [jax.ShapeDtypeStruct((room, UNIT, width), BF16)] * PARTS,
        compiler_params=pltpu.CompilerParams(vmem_limit_bytes=GRANT),
        name="project",
    )(starts, field, straight)


def stiffen(stiff, local, extended, cz):
    cells, nodes, _ = stiff.shape
    breadth = local.shape[2]
    side = extended[2]
    deg = side - 1

    def body(stiff_ref, local_ref, total_ref):
        c = pl.program_id(0)

        @pl.when(c == 0)
        def _():
            total_ref[...] = jnp.zeros_like(total_ref)

        result = jnp.dot(stiff_ref[0], local_ref[0], preferred_element_type=F32)
        u = pl.ds(c // cz * deg, side)
        w = pl.ds(c % cz * deg, side)
        total_ref[u, w] = total_ref[u, w] + result.reshape(side, side, side, breadth)

    shape = extended + (breadth,)
    return pl.pallas_call(
        body,
        grid=(cells,),
        in_specs=[
            pl.BlockSpec((1, nodes, nodes), lambda c: (c, 0, 0)),
            pl.BlockSpec((1, nodes, breadth), lambda c: (c, 0, 0)),
        ],
        out_specs=whole(shape),
        out_shape=jax.ShapeDtypeStruct(shape, F32),
        compiler_params=pltpu.CompilerParams(vmem_limit_bytes=GRANT),
        name="stiffen",
    )(stiff, local)


def merge(incoming, tables, atoms, units, span, after):
    breadth = incoming.shape[2]
    ids, begins, filled, spots, _ = tables
    senders = filled.shape[0]
    each = ids.shape[0] // senders

    def body(ids_ref, begins_ref, filled_ref, spots_ref, incoming_ref, *refs):
        sums_ref, sent_ref = refs[len(after) :]
        sums_ref[...] = jnp.zeros_like(sums_ref)

        def sender(g, carry):
            def add(j, carry):
                slot = g * each + j
                into = pl.ds(ids_ref[slot] * units, units)
                piece = incoming_ref[pl.ds(begins_ref[slot], units)].astype(F32)
                sums_ref[into] = sums_ref[into] + piece
                return carry

            return lax.fori_loop(0, filled_ref[g], add, carry)

        lax.fori_loop(0, senders, sender, 0)

        def pack(a, carry):
            piece = sums_ref[pl.ds(a * units, units)]
            sent_ref[pl.ds(spots_ref[a], units)] = piece.astype(BF16)
            return carry

        lax.fori_loop(0, atoms, pack, 0, unroll=4)

    return pl.pallas_call(
        body,
        in_specs=[smem()] * 4 + [pl.BlockSpec(memory_space=pltpu.VMEM)] + unread(after),
        out_specs=[pl.BlockSpec(memory_space=pltpu.VMEM)] * 2,
        out_shape=[
            jax.ShapeDtypeStruct((atoms * units, UNIT, breadth), F32),
            jax.ShapeDtypeStruct((span, UNIT, breadth), BF16),
        ],
        compiler_params=pltpu.CompilerParams(vmem_limit_bytes=GRANT),
        name="merge",
    )(ids, begins, filled, spots, incoming, *after)


def couple(sums, others, high, low, tables, units, room, after):
    breadth = sums.shape[2]
    groups, edge, _ = high.shape
    ids, begins, filled, spots, shared = tables
    senders = filled.shape[0]
    each = ids.shape[0] // senders
    rows = units * UNIT

    def body(ids_ref, begins_ref, filled_ref, spots_ref, shared_ref, sums_ref, others_ref, *refs):
        high_ref, low_ref = refs[:2]
        out_ref, total_ref, kept_ref = refs[2 + len(after) :]

        def mix(g, carry):
            for m in range(GROUP):
                a = g * GROUP + m
                piece = others_ref[pl.ds(spots_ref[a], units)].astype(F32)
                piece = jnp.where(shared_ref[a] > 0, piece, 0.0)
                piece = sums_ref[pl.ds(a * units, units)] + piece
                total_ref[m * rows : (m + 1) * rows] = piece.reshape(rows, breadth)
            total = total_ref[...]
            upper = total.astype(BF16)
            lower = (total - upper.astype(F32)).astype(BF16)
            mixed = jnp.dot(high_ref[g], upper, preferred_element_type=F32)
            mixed = mixed + jnp.dot(low_ref[g], upper, preferred_element_type=F32)
            mixed = mixed + jnp.dot(high_ref[g], lower, preferred_element_type=F32)
            mixed = mixed.reshape(GROUP * units, UNIT, breadth).astype(BF16)
            kept_ref[pl.ds(g * GROUP * units, GROUP * units)] = mixed
            return carry

        lax.fori_loop(0, groups, mix, 0, unroll=2)

        def sender(g, carry):
            def copy(j, carry):
                slot = g * each + j
                piece = kept_ref[pl.ds(ids_ref[slot] * units, units)]
                out_ref[pl.ds(begins_ref[slot], units)] = piece
                return carry

            return lax.fori_loop(0, filled_ref[g], copy, carry)

        lax.fori_loop(0, senders, sender, 0)

    vmem = pl.BlockSpec(memory_space=pltpu.VMEM)
    return pl.pallas_call(
        body,
        in_specs=[smem()] * 5 + [vmem] * 4 + unread(after),
        out_specs=vmem,
        out_shape=jax.ShapeDtypeStruct((room, UNIT, breadth), BF16),
        scratch_shapes=[
            pltpu.VMEM((edge, breadth), F32),
            pltpu.VMEM((sums.shape[0], UNIT, breadth), BF16),
        ],
        compiler_params=pltpu.CompilerParams(vmem_limit_bytes=GRANT),
        name="couple",
    )(ids, begins, filled, spots, shared, sums, others, high, low, *after)


def apply(turned, answers, begun, starts, used, part, cz, per_atom, after):
    cells, nodes, rows = turned.shape
    breadth = answers.shape[2]
    per_cell = rows // per_atom
    units = per_atom // UNIT
    side = begun.shape[2]
    deg = side - 1

    def body(starts_ref, used_ref, turned_ref, answers_ref, begun_ref, *refs):
        total_ref, stack_ref = refs[len(after) :]
        c = pl.program_id(0)

        @pl.when(c == 0)
        def _():
            total_ref[...] = begun_ref[...]

        row = lax.broadcasted_iota(jnp.int32, (per_atom, breadth), 0)
        for k in range(per_cell):
            entry = c * per_cell + k
            piece = answers_ref[pl.ds(starts_ref[entry], units)].astype(F32)
            piece = piece.reshape(per_atom, breadth)
            piece = jnp.where(row < used_ref[entry] * UNIT, piece, 0.0)
            stack_ref[k * per_atom : (k + 1) * per_atom] = piece.astype(BF16)
        result = jnp.dot(turned_ref[0], stack_ref[...], preferred_element_type=F32)
        u = pl.ds(c // cz * deg, side)
        w = pl.ds(c % cz * deg, side)
        total_ref[u, w] = total_ref[u, w] + result.reshape(side, side, side, breadth)

    shape = begun.shape[:3] + (breadth,)
    return pl.pallas_call(
        body,
        grid=(cells,),
        in_specs=[
            smem(),
            smem(),
            pl.BlockSpec((1, nodes, rows), lambda c: (c, 0, 0)),
            whole(answers.shape),
            pl.BlockSpec(shape, lambda c: (0, 0, 0, part), pipeline_mode=pl.Buffered(1)),
        ]
        + unread(after),
        out_specs=whole(shape),
        out_shape=jax.ShapeDtypeStruct(shape, F32),
        scratch_shapes=[pltpu.VMEM((rows, breadth), BF16)],
        compiler_params=pltpu.CompilerParams(vmem_limit_bytes=GRANT),
        name="apply",
    )(starts, used, turned, answers, begun, *after)


def completed(total):
    span_u, span_w, span_v, breadth = total.shape
    low_v = total[:, :, 0].astype(BF16)
    high_v = total[:, :, -1].astype(BF16)
    from_next = shifted(low_v, ("gy",), (-1,)).astype(F32)[:, :, None]
    from_prev = shifted(high_v, ("gy",), (1,)).astype(F32)[:, :, None]
    gap = jnp.zeros((span_u, span_w, span_v - 2, breadth), F32)
    total = total + jnp.concatenate([from_prev, gap, from_next], axis=2)
    low_u = total[0].astype(BF16)
    high_u = total[-1].astype(BF16)
    from_next = shifted(low_u, ("gx",), (-1,)).astype(F32)[None]
    from_prev = shifted(high_u, ("gx",), (1,)).astype(F32)[None]
    gap = jnp.zeros((span_u - 2, span_w, span_v, breadth), F32)
    return total + jnp.concatenate([from_prev, gap, from_next], axis=0)


def on_device(orbitals, cell_matrices, cell_nodes, projectors, entry_atom, coupling, proj_counts):
    span_x, span_y, layers, _ = orbitals.shape
    matrices = cell_matrices[0, 0]
    node_map = cell_nodes[0, 0]
    cells, per_cell, per_atom, nodes = projectors.shape[2:]
    shapes = projectors[0, 0].reshape(cells, per_cell * per_atom, nodes)
    atom_names = entry_atom[0, 0]
    side = round(nodes ** (1 / 3))
    deg = side - 1
    cz = (layers - 1) // deg
    assert span_y == deg and side**3 == nodes and cells * deg == span_x * cz
    entries = cells * per_cell
    n_gx, n_gy = lax.axis_size("gx"), lax.axis_size("gy")
    devices = n_gx * n_gy
    half = n_gy // 2
    senders = devices // 2
    home_atoms = coupling.shape[0]
    atoms = 2 * home_atoms
    each = 2 * max(2, 2 * entries // devices)
    slots = senders * each
    both = ("gx", "gy")
    teams = [
        [p * n_gy + h * half + r for p in range(n_gx) for r in range(half)] for h in range(2)
    ]

    def exchange(x):
        return lax.all_to_all(
            x, both, split_axis=0, concat_axis=0, axis_index_groups=teams, tiled=True
        )

    units = per_atom // UNIT
    my_x, my_y = lax.axis_index("gx"), lax.axis_index("gy")
    my_half, my_place = my_y // half, my_y % half
    me = my_x * n_gy + my_y
    mine = my_x * half + my_place

    notes = jnp.concatenate([atom_names.reshape(entries), proj_counts])
    notes = jnp.broadcast_to(notes, (devices, entries + home_atoms))
    notes = lax.all_to_all(notes, both, split_axis=0, concat_axis=0, tiled=True)
    names, counts = notes[:, :entries], notes[:, entries:]
    needs = (counts + UNIT - 1) // UNIT
    homes, inner = names // home_atoms, names % home_atoms
    homes_y = homes % n_gy
    at_home = (homes[:, :, None] == jnp.arange(devices)).astype(BF16)
    at_inner = (inner[:, :, None] == jnp.arange(home_atoms)).astype(BF16)
    picked = jnp.einsum("seh,hi->sei", at_home, needs.astype(BF16), preferred_element_type=F32)
    sizes = jnp.sum(picked * at_inner.astype(F32), axis=2).astype(jnp.int32)

    def by_half(x):
        return x.reshape((n_gx, 2, half) + x.shape[1:])

    split = [
        jnp.einsum(
            "seh,sei->hi",
            by_half(at_home)[:, h].reshape((senders,) + at_home.shape[1:]),
            by_half(at_inner)[:, h].reshape((senders,) + at_inner.shape[1:]),
            preferred_element_type=F32,
        )
        for h in range(2)
    ]
    common = ((split[0] > 0) & (split[1] > 0)).astype(jnp.int32)

    order = jnp.arange(entries)[None, :, None]
    present = homes[:, :, None] == jnp.arange(devices)
    sized = sizes[:, :, None]
    loads = jnp.sum(jnp.where(present, sized, 0), axis=1)
    ends = jnp.max(jnp.where(present, order * (2 * units) + sized, 0), axis=1)
    crossing = jnp.sum(common * needs, axis=1)
    table = jnp.concatenate([loads, ends, crossing[None]], axis=0).astype(F32)
    table = table.reshape(2 * devices + 1, n_gx, 2, half)
    lower = table[:, :, 0].reshape(-1, 1, senders)
    turned_to = np.zeros((senders, TURNS * TURNS, senders), np.float32)
    for j, k, p, r in itertools.product(range(TURNS), range(TURNS), range(n_gx), range(half)):
        source = (p + j) % n_gx * half + (r + k) % half
        turned_to[source, j * TURNS + k, p * half + r] = 1.0
    upper = jnp.einsum(
        "ah,hcg->acg",
        table[:, :, 1].reshape(-1, senders),
        jnp.asarray(turned_to),
        precision=lax.Precision.HIGHEST,
    )
    tail = jnp.maximum(lower, upper)[devices : 2 * devices].astype(jnp.int32) % (2 * units)
    joint = (lower + upper).astype(jnp.int32)
    cap = TIGHT * each * units // 64
    span = NARROW * atoms * units // 256
    fullest = jnp.max(joint[:devices] - tail + units, axis=(0, 2))
    widest = jnp.max(joint[-1] + units, axis=1)
    scores = jnp.maximum(fullest * span, widest * cap)
    best = jnp.argmin(scores).astype(jnp.int32)
    fits = jnp.min(scores) <= cap * span
    turn_x, turn_y = best // TURNS, best % TURNS
    over = homes_y // half
    held = over * home_atoms + inner
    places_x = (homes // n_gy - turn_x * over) % n_gx
    places_y = (homes_y % half - turn_y * over) % half
    collectors = places_x * half + places_y

    def of_me(x):
        return lax.dynamic_index_in_dim(x, me, 0, keepdims=False)

    def of_my_half(x):
        x = lax.dynamic_index_in_dim(by_half(x), my_half, 1, keepdims=False)
        return x.reshape((senders,) + x.shape[2:])

    def hosted(x):
        first = my_x * n_gy + my_place
        second = (my_x + turn_x) % n_gx * n_gy + half + (my_place + turn_y) % half
        rows = [lax.dynamic_index_in_dim(x, at, 0, keepdims=False) for at in (first, second)]
        return jnp.concatenate(rows)

    before = jnp.arange(entries)[:, None] < jnp.arange(entries)[None, :]
    own, used = of_me(collectors), of_me(sizes)
    ahead = before & (own[:, None] == own[None, :])
    offsets = jnp.sum(jnp.where(ahead, used[:, None], 0), axis=0)
    theirs = (of_my_half(collectors) == mine).astype(BF16)
    earlier = before.astype(BF16)
    ranks = jnp.dot(theirs, earlier, preferred_element_type=F32).astype(jnp.int32)
    lengths = theirs * of_my_half(sizes).astype(BF16)
    shifts = jnp.dot(lengths, earlier, preferred_element_type=F32).astype(jnp.int32)
    chosen = (ranks[:, None, :] == jnp.arange(each)[:, None]) & (theirs[:, None, :] > 0)
    ids = jnp.sum(jnp.where(chosen, of_my_half(held)[:, None, :], 0), axis=2).reshape(slots)
    places_in = jnp.sum(jnp.where(chosen, shifts[:, None, :], 0), axis=2)
    filled = jnp.sum(theirs.astype(F32), axis=1).astype(jnp.int32)
    shared = hosted(common)
    moved = shared * hosted(needs)
    upto = jnp.arange(atoms)[:, None] < jnp.arange(atoms)[None, :]
    spots = jnp.sum(jnp.where(upto, moved[:, None], 0), axis=0)

    flat = coupling.reshape(-1, 128)
    partner = shifted(flat, ("gy",), (half,))
    lower_mix = jnp.where(my_half > 0, partner, flat)
    upper_mix = jnp.where(my_half > 0, flat, partner)
    choices = [upper_mix] + [shifted(upper_mix, ("gx",), (-j,)) for j in range(1, TURNS)]
    upper_mix = lax.select_n(turn_x, *choices)
    choices = [upper_mix]
    for k in range(1, TURNS):
        pairs = [(h * half + (r + k) % half, h * half + r) for h in range(2) for r in range(half)]
        choices.append(lax.ppermute(upper_mix, "gy", pairs))
    upper_mix = lax.select_n(turn_y, *choices)
    mixers = jnp.concatenate([lower_mix, upper_mix], axis=0).reshape(atoms, per_atom, per_atom)
    active = (jnp.arange(per_atom)[None, :] < hosted(counts)[:, None]).astype(F32)
    mixers = mixers * active[:, :, None] * active[:, None, :]

    cell_ids = jnp.arange(cells, dtype=jnp.int32)[:, None]
    node_w = node_map % layers - cell_ids % cz * deg
    node_v = node_map // layers % (span_y + 1)
    node_u = node_map // (layers * (span_y + 1)) - cell_ids // cz * deg
    places = (node_u * side + node_w) * side + node_v
    stiff, turned, straight = canonical(places, matrices, shapes)

    row_next = shifted(orbitals[:1], ("gx",), (-1,))
    column_next = shifted(orbitals[:, :1], ("gy",), (-1,))
    corner_next = shifted(orbitals[:1, :1], both, (-1, -1))
    widened = jnp.concatenate(
        [
            jnp.concatenate([orbitals, column_next], axis=1),
            jnp.concatenate([row_next, corner_next], axis=1),
        ],
        axis=0,
    )
    grid = jnp.transpose(widened, (0, 2, 1, 3)).astype(F32)
    extended = grid.shape[:3]

    def advance(field, older, mixing, cap, span):
        room = senders * cap
        starts = own * cap + offsets
        begins = (places_in + jnp.arange(senders)[:, None] * cap).reshape(slots)
        tables = (ids, begins, filled, spots, shared)
        local, *outgoing = project(field, straight, starts, room, cz, per_atom)
        if mixing is None:
            mixing = spread(mixers, (local,))
        image = stiffen(stiff, local, extended, cz)
        after = (image,)
        gathered = []
        for packet in outgoing:
            incoming = exchange(packet)
            gathered.append(merge(incoming, tables, atoms, units, span, after))
            after = (gathered[-1][0],)
        answers = []
        for sums, sent in gathered:
            others = shifted(sent, ("gy",), (half,))
            replies = couple(sums, others, *mixing, tables, units, room, after)
            answers.append(exchange(replies))
            after = (replies,)
        totals = []
        for part in range(PARTS):
            totals.append(
                apply(turned, answers[part], image, starts, used, part, cz, per_atom, after)
            )
            after = (totals[-1],)
        image = completed(jnp.concatenate(totals, axis=-1) if PARTS > 1 else totals[0])
        return image if older is None else 2.0 * image - older, mixing

    def packed():
        mixing = None
        older, field = None, grid
        for _ in range(FILTER_DEGREE):
            image, mixing = advance(field, older, mixing, cap, span)
            older, field = field, image
        return field[:span_x, :, :span_y].astype(BF16)

    def roomy():
        mixing = spread(mixers, ())

        def step(at, fields):
            older, field = fields
            image, _ = advance(field, None, mixing, (each + 1) * units, (atoms + 1) * units)
            return field, jnp.where(at == 0, image, 2.0 * image - older)

        fields = (jnp.zeros_like(grid), grid)
        field = lax.fori_loop(0, FILTER_DEGREE, step, fields)[1]
        return field[:span_x, :, :span_y].astype(BF16)

    if MODE == "cond":
        filtered = lax.cond(fits, packed, roomy)
    else:
        filtered = packed() if MODE == "fast" else roomy()
    return jnp.transpose(filtered, (0, 2, 1, 3))


def solution(mesh):
    in_specs = (
        P("gx", "gy", None, None),
        P("gx", "gy", None, None, None),
        P("gx", "gy", None, None),
        P("gx", "gy", None, None, None, None),
        P("gx", "gy", None, None),
        P(("gx", "gy"), None, None),
        P(("gx", "gy")),
    )
    out_specs = P("gx", "gy", None, None)
    return jax.shard_map(
        on_device, mesh=mesh, in_specs=in_specs, out_specs=out_specs, check_vma=False
    )
```

```python
import itertools

import jax
import jax.numpy as jnp
import numpy as np
from jax import lax
from jax.experimental import pallas as pl
from jax.experimental.pallas import tpu as pltpu
from jax.sharding import PartitionSpec as P


FILTER_DEGREE = 3
PARTS = 1
UNIT = 8
TIGHT = 47
NARROW = 172
TURNS = 4
MODE = "cond"
GRANT = 20 * 1024 * 1024
GROUP = 8
BF16 = jnp.bfloat16
F32 = jnp.float32


def shifted(x, axes, by):
    sizes = [lax.axis_size(a) for a in axes]
    pairs = []
    for place in itertools.product(*[range(s) for s in sizes]):
        source = 0
        target = 0
        for at, step, size in zip(place, by, sizes):
            source = source * size + at
            target = target * size + (at + step) % size
        pairs.append((source, target))
    return lax.ppermute(x, axes if len(axes) > 1 else axes[0], pairs)


def whole(shape):
    return pl.BlockSpec(shape, lambda c: (0,) * len(shape), pipeline_mode=pl.Buffered(1))


def smem():
    return pl.BlockSpec(memory_space=pltpu.SMEM)


def unread(after):
    return [pl.BlockSpec(memory_space=pl.ANY)] * len(after)


def canonical(places, matrices, shapes):
    cells, nodes = places.shape
    rows = shapes.shape[1]

    def body(place_ref, matrix_ref, shape_ref, stiff_ref, turned_ref, straight_ref):
        spots = lax.broadcasted_iota(jnp.int32, (nodes, nodes), 0)
        pick = (spots == place_ref[0]).astype(BF16)
        last = (((1,), (1,)), ((), ()))
        half = jnp.dot(pick, matrix_ref[0], preferred_element_type=F32).astype(BF16)
        stiff_ref[0] = lax.dot_general(
            half, pick, last, preferred_element_type=F32
        ).astype(BF16)
        turned_ref[0] = lax.dot_general(
            pick, shape_ref[0], last, preferred_element_type=F32
        ).astype(BF16)
        straight_ref[0] = lax.dot_general(
            shape_ref[0], pick, last, preferred_element_type=F32
        ).astype(BF16)

    return pl.pallas_call(
        body,
        grid=(cells,),
        in_specs=[
            pl.BlockSpec((1, 1, nodes), lambda c: (c, 0, 0)),
            pl.BlockSpec((1, nodes, nodes), lambda c: (c, 0, 0)),
            pl.BlockSpec((1, rows, nodes), lambda c: (c, 0, 0)),
        ],
        out_specs=[
            pl.BlockSpec((1, nodes, nodes), lambda c: (c, 0, 0)),
            pl.BlockSpec((1, nodes, rows), lambda c: (c, 0, 0)),
            pl.BlockSpec((1, rows, nodes), lambda c: (c, 0, 0)),
        ],
        out_shape=[
            jax.ShapeDtypeStruct((cells, nodes, nodes), BF16),
            jax.ShapeDtypeStruct((cells, nodes, rows), BF16),
            jax.ShapeDtypeStruct((cells, rows, nodes), BF16),
        ],
        compiler_params=pltpu.CompilerParams(vmem_limit_bytes=GRANT),
        name="canonical",
    )(places.reshape(cells, 1, nodes), matrices, shapes)


def spread(mixers, after):
    atoms, per_atom, _ = mixers.shape
    groups = atoms // GROUP
    edge = GROUP * per_atom

    def body(mixers_ref, *refs):
        high_ref, low_ref = refs[len(after) :]
        rows = lax.broadcasted_iota(jnp.int32, (edge, edge), 0) // per_atom
        columns = lax.broadcasted_iota(jnp.int32, (edge, edge), 1) // per_atom

        def one(g, carry):
            block = mixers_ref[pl.ds(g * GROUP, GROUP)].reshape(edge, per_atom)
            block = jnp.concatenate([block] * GROUP, axis=1)
            block = jnp.where(rows == columns, block, 0.0)
            high = block.astype(BF16)
            high_ref[g] = high
            low_ref[g] = (block - high.astype(F32)).astype(BF16)
            return carry

        lax.fori_loop(0, groups, one, 0)

    vmem = pl.BlockSpec(memory_space=pltpu.VMEM)
    return pl.pallas_call(
        body,
        in_specs=[vmem] + unread(after),
        out_specs=[vmem, vmem],
        out_shape=[jax.ShapeDtypeStruct((groups, edge, edge), BF16)] * 2,
        compiler_params=pltpu.CompilerParams(vmem_limit_bytes=GRANT),
        name="spread",
    )(mixers, *after)


def project(field, straight, starts, room, cz, per_atom):
    cells, rows, nodes = straight.shape
    side = field.shape[2]
    deg = side - 1
    breadth = field.shape[3]
    per_cell = rows // per_atom
    width = breadth // PARTS
    units = per_atom // UNIT

    def body(starts_ref, field_ref, straight_ref, local_ref, *out_refs):
        c = pl.program_id(0)
        u = c // cz * deg
        w = c % cz * deg
        block = field_ref[pl.ds(u, side), pl.ds(w, side)]
        local = block.reshape(nodes, breadth).astype(BF16)
        local_ref[0] = local
        values = jnp.dot(straight_ref[0], local, preferred_element_type=F32)
        for k in range(per_cell):
            start = starts_ref[c * per_cell + k]
            for s, out_ref in enumerate(out_refs):
                piece = values[k * per_atom : (k + 1) * per_atom, s * width : (s + 1) * width]
                out_ref[pl.ds(start, units)] = piece.reshape(units, UNIT, width).astype(BF16)

    return pl.pallas_call(
        body,
        grid=(cells,),
        in_specs=[
            smem(),
            whole(field.shape),
            pl.BlockSpec((1, rows, nodes), lambda c: (c, 0, 0)),
        ],
        out_specs=[
            pl.BlockSpec((1, nodes, breadth), lambda c: (c, 0, 0)),
        ]
        + [whole((room, UNIT, width))] * PARTS,
        out_shape=[
            jax.ShapeDtypeStruct((cells, nodes, breadth), BF16),
        ]
        + [jax.ShapeDtypeStruct((room, UNIT, width), BF16)] * PARTS,
        compiler_params=pltpu.CompilerParams(vmem_limit_bytes=GRANT),
        name="project",
    )(starts, field, straight)


def stiffen(stiff, local, extended, cz):
    cells, nodes, _ = stiff.shape
    breadth = local.shape[2]
    side = extended[2]
    deg = side - 1

    def body(stiff_ref, local_ref, total_ref):
        c = pl.program_id(0)

        @pl.when(c == 0)
        def _():
            total_ref[...] = jnp.zeros_like(total_ref)

        result = jnp.dot(stiff_ref[0], local_ref[0], preferred_element_type=F32)
        u = pl.ds(c // cz * deg, side)
        w = pl.ds(c % cz * deg, side)
        total_ref[u, w] = total_ref[u, w] + result.reshape(side, side, side, breadth)

    shape = extended + (breadth,)
    return pl.pallas_call(
        body,
        grid=(cells,),
        in_specs=[
            pl.BlockSpec((1, nodes, nodes), lambda c: (c, 0, 0)),
            pl.BlockSpec((1, nodes, breadth), lambda c: (c, 0, 0)),
        ],
        out_specs=whole(shape),
        out_shape=jax.ShapeDtypeStruct(shape, F32),
        compiler_params=pltpu.CompilerParams(vmem_limit_bytes=GRANT),
        name="stiffen",
    )(stiff, local)


def merge(incoming, tables, atoms, units, span, after):
    breadth = incoming.shape[2]
    ids, begins, filled, spots, _ = tables
    senders = filled.shape[0]
    each = ids.shape[0] // senders

    def body(ids_ref, begins_ref, filled_ref, spots_ref, incoming_ref, *refs):
        sums_ref, sent_ref = refs[len(after) :]
        sums_ref[...] = jnp.zeros_like(sums_ref)

        def sender(g, carry):
            def add(j, carry):
                slot = g * each + j
                into = pl.ds(ids_ref[slot] * units, units)
                piece = incoming_ref[pl.ds(begins_ref[slot], units)].astype(F32)
                sums_ref[into] = sums_ref[into] + piece
                return carry

            return lax.fori_loop(0, filled_ref[g], add, carry)

        lax.fori_loop(0, senders, sender, 0)

        def pack(a, carry):
            piece = sums_ref[pl.ds(a * units, units)]
            sent_ref[pl.ds(spots_ref[a], units)] = piece.astype(BF16)
            return carry

        lax.fori_loop(0, atoms, pack, 0, unroll=4)

    return pl.pallas_call(
        body,
        in_specs=[smem()] * 4 + [pl.BlockSpec(memory_space=pltpu.VMEM)] + unread(after),
        out_specs=[pl.BlockSpec(memory_space=pltpu.VMEM)] * 2,
        out_shape=[
            jax.ShapeDtypeStruct((atoms * units, UNIT, breadth), F32),
            jax.ShapeDtypeStruct((span, UNIT, breadth), BF16),
        ],
        compiler_params=pltpu.CompilerParams(vmem_limit_bytes=GRANT),
        name="merge",
    )(ids, begins, filled, spots, incoming, *after)


def couple(sums, others, high, low, tables, units, room, after):
    breadth = sums.shape[2]
    groups, edge, _ = high.shape
    ids, begins, filled, spots, shared = tables
    senders = filled.shape[0]
    each = ids.shape[0] // senders
    rows = units * UNIT

    def body(ids_ref, begins_ref, filled_ref, spots_ref, shared_ref, sums_ref, others_ref, *refs):
        high_ref, low_ref = refs[:2]
        out_ref, total_ref, kept_ref = refs[2 + len(after) :]

        def mix(g, carry):
            for m in range(GROUP):
                a = g * GROUP + m
                piece = others_ref[pl.ds(spots_ref[a], units)].astype(F32)
                piece = jnp.where(shared_ref[a] > 0, piece, 0.0)
                piece = sums_ref[pl.ds(a * units, units)] + piece
                total_ref[m * rows : (m + 1) * rows] = piece.reshape(rows, breadth)
            total = total_ref[...]
            upper = total.astype(BF16)
            lower = (total - upper.astype(F32)).astype(BF16)
            mixed = jnp.dot(high_ref[g], upper, preferred_element_type=F32)
            mixed = mixed + jnp.dot(low_ref[g], upper, preferred_element_type=F32)
            mixed = mixed + jnp.dot(high_ref[g], lower, preferred_element_type=F32)
            mixed = mixed.reshape(GROUP * units, UNIT, breadth).astype(BF16)
            kept_ref[pl.ds(g * GROUP * units, GROUP * units)] = mixed
            return carry

        lax.fori_loop(0, groups, mix, 0, unroll=2)

        def sender(g, carry):
            def copy(j, carry):
                slot = g * each + j
                piece = kept_ref[pl.ds(ids_ref[slot] * units, units)]
                out_ref[pl.ds(begins_ref[slot], units)] = piece
                return carry

            return lax.fori_loop(0, filled_ref[g], copy, carry)

        lax.fori_loop(0, senders, sender, 0)

    vmem = pl.BlockSpec(memory_space=pltpu.VMEM)
    return pl.pallas_call(
        body,
        in_specs=[smem()] * 5 + [vmem] * 4 + unread(after),
        out_specs=vmem,
        out_shape=jax.ShapeDtypeStruct((room, UNIT, breadth), BF16),
        scratch_shapes=[
            pltpu.VMEM((edge, breadth), F32),
            pltpu.VMEM((sums.shape[0], UNIT, breadth), BF16),
        ],
        compiler_params=pltpu.CompilerParams(vmem_limit_bytes=GRANT),
        name="couple",
    )(ids, begins, filled, spots, shared, sums, others, high, low, *after)


def apply(turned, answers, begun, starts, used, part, cz, per_atom, after):
    cells, nodes, rows = turned.shape
    breadth = answers.shape[2]
    per_cell = rows // per_atom
    units = per_atom // UNIT
    side = begun.shape[2]
    deg = side - 1

    def body(starts_ref, used_ref, turned_ref, answers_ref, begun_ref, *refs):
        total_ref, stack_ref = refs[len(after) :]
        c = pl.program_id(0)

        @pl.when(c == 0)
        def _():
            total_ref[...] = begun_ref[...]

        row = lax.broadcasted_iota(jnp.int32, (per_atom, breadth), 0)
        for k in range(per_cell):
            entry = c * per_cell + k
            piece = answers_ref[pl.ds(starts_ref[entry], units)].astype(F32)
            piece = piece.reshape(per_atom, breadth)
            piece = jnp.where(row < used_ref[entry] * UNIT, piece, 0.0)
            stack_ref[k * per_atom : (k + 1) * per_atom] = piece.astype(BF16)
        result = jnp.dot(turned_ref[0], stack_ref[...], preferred_element_type=F32)
        u = pl.ds(c // cz * deg, side)
        w = pl.ds(c % cz * deg, side)
        total_ref[u, w] = total_ref[u, w] + result.reshape(side, side, side, breadth)

    shape = begun.shape[:3] + (breadth,)
    return pl.pallas_call(
        body,
        grid=(cells,),
        in_specs=[
            smem(),
            smem(),
            pl.BlockSpec((1, nodes, rows), lambda c: (c, 0, 0)),
            whole(answers.shape),
            pl.BlockSpec(shape, lambda c: (0, 0, 0, part), pipeline_mode=pl.Buffered(1)),
        ]
        + unread(after),
        out_specs=whole(shape),
        out_shape=jax.ShapeDtypeStruct(shape, F32),
        scratch_shapes=[pltpu.VMEM((rows, breadth), BF16)],
        compiler_params=pltpu.CompilerParams(vmem_limit_bytes=GRANT),
        name="apply",
    )(starts, used, turned, answers, begun, *after)


def finish(total, sides, ends, scale, older):
    span_u, span_w, span_v, breadth = total.shape

    def body(scale_ref, total_ref, prev_v_ref, next_v_ref, prev_u_ref, next_u_ref, *refs):
        out_ref = refs[-1]
        times = scale_ref[0]
        at = lax.broadcasted_iota(jnp.int32, (span_w, span_v, breadth), 1)

        def row(u, carry):
            first = prev_v_ref[u].astype(F32)[:, None]
            last = next_v_ref[u].astype(F32)[:, None]
            value = total_ref[u] + jnp.where(at == 0, first, 0.0)
            value = times * (value + jnp.where(at == span_v - 1, last, 0.0))
            if older is not None:
                value = value - refs[0][u]
            out_ref[u] = value
            return carry

        lax.fori_loop(0, span_u, row, 0)
        out_ref[0] = out_ref[0] + times * prev_u_ref[...].astype(F32)
        out_ref[span_u - 1] = out_ref[span_u - 1] + times * next_u_ref[...].astype(F32)

    vmem = pl.BlockSpec(memory_space=pltpu.VMEM)
    known = [] if older is None else [older]
    return pl.pallas_call(
        body,
        in_specs=[smem()] + [vmem] * (5 + len(known)),
        out_specs=vmem,
        out_shape=jax.ShapeDtypeStruct(total.shape, F32),
        compiler_params=pltpu.CompilerParams(vmem_limit_bytes=GRANT),
        name="finish",
    )(scale, total, *sides, *ends, *known)


def completed(total, scale, older):
    low_v = total[:, :, 0].astype(BF16)
    high_v = total[:, :, -1].astype(BF16)
    next_v = shifted(low_v, ("gy",), (-1,))
    prev_v = shifted(high_v, ("gy",), (1,))

    def edge(u):
        row = total[u]
        first = row[:, :1] + prev_v[u][:, None].astype(F32)
        last = row[:, -1:] + next_v[u][:, None].astype(F32)
        return jnp.concatenate([first, row[:, 1:-1], last], axis=1).astype(BF16)

    next_u = shifted(edge(0), ("gx",), (-1,))
    prev_u = shifted(edge(-1), ("gx",), (1,))
    return finish(total, (prev_v, next_v), (prev_u, next_u), scale, older)


def on_device(orbitals, cell_matrices, cell_nodes, projectors, entry_atom, coupling, proj_counts):
    span_x, span_y, layers, _ = orbitals.shape
    matrices = cell_matrices[0, 0]
    node_map = cell_nodes[0, 0]
    cells, per_cell, per_atom, nodes = projectors.shape[2:]
    shapes = projectors[0, 0].reshape(cells, per_cell * per_atom, nodes)
    atom_names = entry_atom[0, 0]
    side = round(nodes ** (1 / 3))
    deg = side - 1
    cz = (layers - 1) // deg
    assert span_y == deg and side**3 == nodes and cells * deg == span_x * cz
    entries = cells * per_cell
    n_gx, n_gy = lax.axis_size("gx"), lax.axis_size("gy")
    devices = n_gx * n_gy
    half = n_gy // 2
    senders = devices // 2
    home_atoms = coupling.shape[0]
    atoms = 2 * home_atoms
    each = 2 * max(2, 2 * entries // devices)
    slots = senders * each
    both = ("gx", "gy")
    teams = [
        [p * n_gy + h * half + r for p in range(n_gx) for r in range(half)] for h in range(2)
    ]

    def exchange(x):
        return lax.all_to_all(
            x, both, split_axis=0, concat_axis=0, axis_index_groups=teams, tiled=True
        )

    units = per_atom // UNIT
    my_x, my_y = lax.axis_index("gx"), lax.axis_index("gy")
    my_half, my_place = my_y // half, my_y % half
    me = my_x * n_gy + my_y
    mine = my_x * half + my_place

    notes = jnp.concatenate([atom_names.reshape(entries), proj_counts])
    notes = jnp.broadcast_to(notes, (devices, entries + home_atoms))
    notes = lax.all_to_all(notes, both, split_axis=0, concat_axis=0, tiled=True)
    names, counts = notes[:, :entries], notes[:, entries:]
    needs = (counts + UNIT - 1) // UNIT
    homes, inner = names // home_atoms, names % home_atoms
    homes_y = homes % n_gy
    at_home = (homes[:, :, None] == jnp.arange(devices)).astype(BF16)
    at_inner = (inner[:, :, None] == jnp.arange(home_atoms)).astype(BF16)
    picked = jnp.einsum("seh,hi->sei", at_home, needs.astype(BF16), preferred_element_type=F32)
    sizes = jnp.sum(picked * at_inner.astype(F32), axis=2).astype(jnp.int32)

    def by_half(x):
        return x.reshape((n_gx, 2, half) + x.shape[1:])

    split = [
        jnp.einsum(
            "seh,sei->hi",
            by_half(at_home)[:, h].reshape((senders,) + at_home.shape[1:]),
            by_half(at_inner)[:, h].reshape((senders,) + at_inner.shape[1:]),
            preferred_element_type=F32,
        )
        for h in range(2)
    ]
    common = ((split[0] > 0) & (split[1] > 0)).astype(jnp.int32)

    order = jnp.arange(entries)[None, :, None]
    present = homes[:, :, None] == jnp.arange(devices)
    sized = sizes[:, :, None]
    loads = jnp.sum(jnp.where(present, sized, 0), axis=1)
    ends = jnp.max(jnp.where(present, order * (2 * units) + sized, 0), axis=1)
    crossing = jnp.sum(common * needs, axis=1)
    table = jnp.concatenate([loads, ends, crossing[None]], axis=0).astype(F32)
    table = table.reshape(2 * devices + 1, n_gx, 2, half)
    lower = table[:, :, 0].reshape(-1, 1, senders)
    turned_to = np.zeros((senders, TURNS * TURNS, senders), np.float32)
    for j, k, p, r in itertools.product(range(TURNS), range(TURNS), range(n_gx), range(half)):
        source = (p + j) % n_gx * half + (r + k) % half
        turned_to[source, j * TURNS + k, p * half + r] = 1.0
    upper = jnp.einsum(
        "ah,hcg->acg",
        table[:, :, 1].reshape(-1, senders),
        jnp.asarray(turned_to),
        precision=lax.Precision.HIGHEST,
    )
    tail = jnp.maximum(lower, upper)[devices : 2 * devices].astype(jnp.int32) % (2 * units)
    joint = (lower + upper).astype(jnp.int32)
    cap = TIGHT * each * units // 64
    span = NARROW * atoms * units // 256
    fullest = jnp.max(joint[:devices] - tail + units, axis=(0, 2))
    widest = jnp.max(joint[-1] + units, axis=1)
    scores = jnp.maximum(fullest * span, widest * cap)
    best = jnp.argmin(scores).astype(jnp.int32)
    fits = jnp.min(scores) <= cap * span
    turn_x, turn_y = best // TURNS, best % TURNS
    over = homes_y // half
    held = over * home_atoms + inner
    places_x = (homes // n_gy - turn_x * over) % n_gx
    places_y = (homes_y % half - turn_y * over) % half
    collectors = places_x * half + places_y

    def of_me(x):
        return lax.dynamic_index_in_dim(x, me, 0, keepdims=False)

    def of_my_half(x):
        x = lax.dynamic_index_in_dim(by_half(x), my_half, 1, keepdims=False)
        return x.reshape((senders,) + x.shape[2:])

    def hosted(x):
        first = my_x * n_gy + my_place
        second = (my_x + turn_x) % n_gx * n_gy + half + (my_place + turn_y) % half
        rows = [lax.dynamic_index_in_dim(x, at, 0, keepdims=False) for at in (first, second)]
        return jnp.concatenate(rows)

    before = jnp.arange(entries)[:, None] < jnp.arange(entries)[None, :]
    own, used = of_me(collectors), of_me(sizes)
    ahead = before & (own[:, None] == own[None, :])
    offsets = jnp.sum(jnp.where(ahead, used[:, None], 0), axis=0)
    theirs = (of_my_half(collectors) == mine).astype(BF16)
    earlier = before.astype(BF16)
    ranks = jnp.dot(theirs, earlier, preferred_element_type=F32).astype(jnp.int32)
    lengths = theirs * of_my_half(sizes).astype(BF16)
    shifts = jnp.dot(lengths, earlier, preferred_element_type=F32).astype(jnp.int32)
    chosen = (ranks[:, None, :] == jnp.arange(each)[:, None]) & (theirs[:, None, :] > 0)
    ids = jnp.sum(jnp.where(chosen, of_my_half(held)[:, None, :], 0), axis=2).reshape(slots)
    places_in = jnp.sum(jnp.where(chosen, shifts[:, None, :], 0), axis=2)
    filled = jnp.sum(theirs.astype(F32), axis=1).astype(jnp.int32)
    shared = hosted(common)
    moved = shared * hosted(needs)
    upto = jnp.arange(atoms)[:, None] < jnp.arange(atoms)[None, :]
    spots = jnp.sum(jnp.where(upto, moved[:, None], 0), axis=0)

    flat = coupling.reshape(-1, 128)
    partner = shifted(flat, ("gy",), (half,))
    lower_mix = jnp.where(my_half > 0, partner, flat)
    upper_mix = jnp.where(my_half > 0, flat, partner)
    choices = [upper_mix] + [shifted(upper_mix, ("gx",), (-j,)) for j in range(1, TURNS)]
    upper_mix = lax.select_n(turn_x, *choices)
    choices = [upper_mix]
    for k in range(1, TURNS):
        pairs = [(h * half + (r + k) % half, h * half + r) for h in range(2) for r in range(half)]
        choices.append(lax.ppermute(upper_mix, "gy", pairs))
    upper_mix = lax.select_n(turn_y, *choices)
    mixers = jnp.concatenate([lower_mix, upper_mix], axis=0).reshape(atoms, per_atom, per_atom)
    active = (jnp.arange(per_atom)[None, :] < hosted(counts)[:, None]).astype(F32)
    mixers = mixers * active[:, :, None] * active[:, None, :]

    cell_ids = jnp.arange(cells, dtype=jnp.int32)[:, None]
    node_w = node_map % layers - cell_ids % cz * deg
    node_v = node_map // layers % (span_y + 1)
    node_u = node_map // (layers * (span_y + 1)) - cell_ids // cz * deg
    places = (node_u * side + node_w) * side + node_v
    stiff, turned, straight = canonical(places, matrices, shapes)

    row_next = shifted(orbitals[:1], ("gx",), (-1,))
    column_next = shifted(orbitals[:, :1], ("gy",), (-1,))
    corner_next = shifted(orbitals[:1, :1], both, (-1, -1))
    widened = jnp.concatenate(
        [
            jnp.concatenate([orbitals, column_next], axis=1),
            jnp.concatenate([row_next, corner_next], axis=1),
        ],
        axis=0,
    )
    grid = jnp.transpose(widened, (0, 2, 1, 3)).astype(F32)
    extended = grid.shape[:3]

    def advance(field, older, scale, mixing, cap, span):
        room = senders * cap
        starts = own * cap + offsets
        begins = (places_in + jnp.arange(senders)[:, None] * cap).reshape(slots)
        tables = (ids, begins, filled, spots, shared)
        local, *outgoing = project(field, straight, starts, room, cz, per_atom)
        if mixing is None:
            mixing = spread(mixers, (local,))
        image = stiffen(stiff, local, extended, cz)
        after = (image,)
        gathered = []
        for packet in outgoing:
            incoming = exchange(packet)
            gathered.append(merge(incoming, tables, atoms, units, span, after))
            after = (gathered[-1][0],)
        answers = []
        for sums, sent in gathered:
            others = shifted(sent, ("gy",), (half,))
            replies = couple(sums, others, *mixing, tables, units, room, after)
            answers.append(exchange(replies))
            after = (replies,)
        totals = []
        for part in range(PARTS):
            totals.append(
                apply(turned, answers[part], image, starts, used, part, cz, per_atom, after)
            )
            after = (totals[-1],)
        total = jnp.concatenate(totals, axis=-1) if PARTS > 1 else totals[0]
        return completed(total, scale, older), mixing

    def packed():
        mixing = None
        older, field = None, grid
        for step in range(FILTER_DEGREE):
            scale = jnp.full((1,), 1.0 if step == 0 else 2.0, F32)
            image, mixing = advance(field, older, scale, mixing, cap, span)
            older, field = field, image
        return field[:span_x, :, :span_y].astype(BF16)

    def roomy():
        mixing = spread(mixers, ())

        def step(at, fields):
            older, field = fields
            scale = jnp.where(at == 0, 1.0, 2.0).astype(F32).reshape(1)
            image, _ = advance(
                field, older, scale, mixing, (each + 1) * units, (atoms + 1) * units
            )
            return field, image

        fields = (jnp.zeros_like(grid), grid)
        field = lax.fori_loop(0, FILTER_DEGREE, step, fields)[1]
        return field[:span_x, :, :span_y].astype(BF16)

    if MODE == "cond":
        filtered = lax.cond(fits, packed, roomy)
    else:
        filtered = packed() if MODE == "fast" else roomy()
    return jnp.transpose(filtered, (0, 2, 1, 3))


def solution(mesh):
    in_specs = (
        P("gx", "gy", None, None),
        P("gx", "gy", None, None, None),
        P("gx", "gy", None, None),
        P("gx", "gy", None, None, None, None),
        P("gx", "gy", None, None),
        P(("gx", "gy"), None, None),
        P(("gx", "gy")),
    )
    out_specs = P("gx", "gy", None, None)
    return jax.shard_map(
        on_device, mesh=mesh, in_specs=in_specs, out_specs=out_specs, check_vma=False
    )
```

```python
import itertools

import jax
import jax.numpy as jnp
import numpy as np
from jax import lax
from jax.experimental import pallas as pl
from jax.experimental.pallas import tpu as pltpu
from jax.sharding import PartitionSpec as P


FILTER_DEGREE = 3
PARTS = 1
UNIT = 8
TIGHT = 47
NARROW = 172
TURNS = 4
MODE = "cond"
GRANT = 20 * 1024 * 1024
GROUP = 8
BF16 = jnp.bfloat16
F32 = jnp.float32


def shifted(x, axes, by):
    sizes = [lax.axis_size(a) for a in axes]
    pairs = []
    for place in itertools.product(*[range(s) for s in sizes]):
        source = 0
        target = 0
        for at, step, size in zip(place, by, sizes):
            source = source * size + at
            target = target * size + (at + step) % size
        pairs.append((source, target))
    return lax.ppermute(x, axes if len(axes) > 1 else axes[0], pairs)


def whole(shape):
    return pl.BlockSpec(shape, lambda c: (0,) * len(shape), pipeline_mode=pl.Buffered(1))


def smem():
    return pl.BlockSpec(memory_space=pltpu.SMEM)


def unread(after):
    return [pl.BlockSpec(memory_space=pl.ANY)] * len(after)


def pick_matrix(place_ref, nodes):
    spots = lax.broadcasted_iota(jnp.int32, (nodes, nodes), 0)
    return (spots == place_ref[0]).astype(BF16)


LAST = (((1,), (1,)), ((), ()))


def canonical(places, matrices, shapes, after):
    cells, rows, nodes = shapes.shape

    def body(place_ref, matrix_ref, shape_ref, *refs):
        stiff_ref, turned_ref = refs[len(after) :]
        pick = pick_matrix(place_ref, nodes)
        half = jnp.dot(pick, matrix_ref[0], preferred_element_type=F32).astype(BF16)
        full = lax.dot_general(half, pick, LAST, preferred_element_type=F32)
        stiff_ref[0] = full.astype(BF16)
        flipped = lax.dot_general(pick, shape_ref[0], LAST, preferred_element_type=F32)
        turned_ref[0] = flipped.astype(BF16)

    def block(shape):
        return pl.BlockSpec((1,) + shape, lambda c: (c, 0, 0))

    return pl.pallas_call(
        body,
        grid=(cells,),
        in_specs=[block((1, nodes)), block((nodes, nodes)), block((rows, nodes))] + unread(after),
        out_specs=[block((nodes, nodes)), block((nodes, rows))],
        out_shape=[
            jax.ShapeDtypeStruct((cells, nodes, nodes), BF16),
            jax.ShapeDtypeStruct((cells, nodes, rows), BF16),
        ],
        compiler_params=pltpu.CompilerParams(vmem_limit_bytes=GRANT),
        name="canonical",
    )(places, matrices, shapes, *after)


def spread(mixers, after):
    atoms, per_atom, _ = mixers.shape
    groups = atoms // GROUP
    edge = GROUP * per_atom

    def body(mixers_ref, *refs):
        high_ref, low_ref = refs[len(after) :]
        rows = lax.broadcasted_iota(jnp.int32, (edge, edge), 0) // per_atom
        columns = lax.broadcasted_iota(jnp.int32, (edge, edge), 1) // per_atom

        def one(g, carry):
            block = mixers_ref[pl.ds(g * GROUP, GROUP)].reshape(edge, per_atom)
            block = jnp.concatenate([block] * GROUP, axis=1)
            block = jnp.where(rows == columns, block, 0.0)
            high = block.astype(BF16)
            high_ref[g] = high
            low_ref[g] = (block - high.astype(F32)).astype(BF16)
            return carry

        lax.fori_loop(0, groups, one, 0)

    vmem = pl.BlockSpec(memory_space=pltpu.VMEM)
    return pl.pallas_call(
        body,
        in_specs=[vmem] + unread(after),
        out_specs=[vmem, vmem],
        out_shape=[jax.ShapeDtypeStruct((groups, edge, edge), BF16)] * 2,
        compiler_params=pltpu.CompilerParams(vmem_limit_bytes=GRANT),
        name="spread",
    )(mixers, *after)


def project(field, straight, starts, room, cz, per_atom, places=None):
    cells, rows, nodes = straight.shape
    side = field.shape[2]
    deg = side - 1
    breadth = field.shape[3]
    per_cell = rows // per_atom
    width = breadth // PARTS
    units = per_atom // UNIT
    raw = places is not None

    def body(starts_ref, field_ref, straight_ref, *refs):
        if raw:
            place_ref, grid_ref, *refs = refs
        local_ref, *out_refs = refs
        c = pl.program_id(0)
        u = c // cz * deg
        w = c % cz * deg
        block = field_ref[pl.ds(u, side), pl.ds(w, side)]
        local = block.reshape(nodes, breadth).astype(BF16)
        local_ref[0] = local
        rows_of = straight_ref[0]
        if raw:
            pick = pick_matrix(place_ref, nodes)
            rows_of = lax.dot_general(rows_of, pick, LAST, preferred_element_type=F32)
            rows_of = rows_of.astype(BF16)
            grid_ref[0] = rows_of
        values = jnp.dot(rows_of, local, preferred_element_type=F32)
        for k in range(per_cell):
            start = starts_ref[c * per_cell + k]
            for s, out_ref in enumerate(out_refs):
                piece = values[k * per_atom : (k + 1) * per_atom, s * width : (s + 1) * width]
                out_ref[pl.ds(start, units)] = piece.reshape(units, UNIT, width).astype(BF16)

    def block(shape):
        return pl.BlockSpec((1,) + shape, lambda c: (c, 0, 0))

    turning = [jax.ShapeDtypeStruct(straight.shape, BF16)] if raw else []
    return pl.pallas_call(
        body,
        grid=(cells,),
        in_specs=[smem(), whole(field.shape), block((rows, nodes))]
        + ([block((1, nodes))] if raw else []),
        out_specs=([block((rows, nodes))] if raw else [])
        + [block((nodes, breadth))]
        + [whole((room, UNIT, width))] * PARTS,
        out_shape=turning
        + [jax.ShapeDtypeStruct((cells, nodes, breadth), BF16)]
        + [jax.ShapeDtypeStruct((room, UNIT, width), BF16)] * PARTS,
        compiler_params=pltpu.CompilerParams(vmem_limit_bytes=GRANT),
        name="project",
    )(starts, field, straight, *([places] if raw else []))


def stiffen(stiff, local, extended, cz):
    cells, nodes, _ = stiff.shape
    breadth = local.shape[2]
    side = extended[2]
    deg = side - 1

    def body(stiff_ref, local_ref, total_ref):
        c = pl.program_id(0)

        @pl.when(c == 0)
        def _():
            total_ref[...] = jnp.zeros_like(total_ref)

        result = jnp.dot(stiff_ref[0], local_ref[0], preferred_element_type=F32)
        u = pl.ds(c // cz * deg, side)
        w = pl.ds(c % cz * deg, side)
        total_ref[u, w] = total_ref[u, w] + result.reshape(side, side, side, breadth)

    shape = extended + (breadth,)
    return pl.pallas_call(
        body,
        grid=(cells,),
        in_specs=[
            pl.BlockSpec((1, nodes, nodes), lambda c: (c, 0, 0)),
            pl.BlockSpec((1, nodes, breadth), lambda c: (c, 0, 0)),
        ],
        out_specs=whole(shape),
        out_shape=jax.ShapeDtypeStruct(shape, F32),
        compiler_params=pltpu.CompilerParams(vmem_limit_bytes=GRANT),
        name="stiffen",
    )(stiff, local)


def merge(incoming, tables, atoms, units, span, after):
    breadth = incoming.shape[2]
    ids, begins, filled, spots, _ = tables
    senders = filled.shape[0]
    each = ids.shape[0] // senders

    def body(ids_ref, begins_ref, filled_ref, spots_ref, incoming_ref, *refs):
        sums_ref, sent_ref = refs[len(after) :]
        sums_ref[...] = jnp.zeros_like(sums_ref)

        def sender(g, carry):
            def add(j, carry):
                slot = g * each + j
                into = pl.ds(ids_ref[slot] * units, units)
                piece = incoming_ref[pl.ds(begins_ref[slot], units)].astype(F32)
                sums_ref[into] = sums_ref[into] + piece
                return carry

            return lax.fori_loop(0, filled_ref[g], add, carry)

        lax.fori_loop(0, senders, sender, 0)

        def pack(a, carry):
            piece = sums_ref[pl.ds(a * units, units)]
            sent_ref[pl.ds(spots_ref[a], units)] = piece.astype(BF16)
            return carry

        lax.fori_loop(0, atoms, pack, 0, unroll=4)

    return pl.pallas_call(
        body,
        in_specs=[smem()] * 4 + [pl.BlockSpec(memory_space=pltpu.VMEM)] + unread(after),
        out_specs=[pl.BlockSpec(memory_space=pltpu.VMEM)] * 2,
        out_shape=[
            jax.ShapeDtypeStruct((atoms * units, UNIT, breadth), F32),
            jax.ShapeDtypeStruct((span, UNIT, breadth), BF16),
        ],
        compiler_params=pltpu.CompilerParams(vmem_limit_bytes=GRANT),
        name="merge",
    )(ids, begins, filled, spots, incoming, *after)


def couple(sums, others, high, low, tables, units, room, after):
    breadth = sums.shape[2]
    groups, edge, _ = high.shape
    ids, begins, filled, spots, shared = tables
    senders = filled.shape[0]
    each = ids.shape[0] // senders
    rows = units * UNIT

    def body(ids_ref, begins_ref, filled_ref, spots_ref, shared_ref, sums_ref, others_ref, *refs):
        high_ref, low_ref = refs[:2]
        out_ref, total_ref, kept_ref = refs[2 + len(after) :]

        def mix(g, carry):
            for m in range(GROUP):
                a = g * GROUP + m
                piece = others_ref[pl.ds(spots_ref[a], units)].astype(F32)
                piece = jnp.where(shared_ref[a] > 0, piece, 0.0)
                piece = sums_ref[pl.ds(a * units, units)] + piece
                total_ref[m * rows : (m + 1) * rows] = piece.reshape(rows, breadth)
            total = total_ref[...]
            upper = total.astype(BF16)
            lower = (total - upper.astype(F32)).astype(BF16)
            mixed = jnp.dot(high_ref[g], upper, preferred_element_type=F32)
            mixed = mixed + jnp.dot(low_ref[g], upper, preferred_element_type=F32)
            mixed = mixed + jnp.dot(high_ref[g], lower, preferred_element_type=F32)
            mixed = mixed.reshape(GROUP * units, UNIT, breadth).astype(BF16)
            kept_ref[pl.ds(g * GROUP * units, GROUP * units)] = mixed
            return carry

        lax.fori_loop(0, groups, mix, 0, unroll=2)

        def sender(g, carry):
            def copy(j, carry):
                slot = g * each + j
                piece = kept_ref[pl.ds(ids_ref[slot] * units, units)]
                out_ref[pl.ds(begins_ref[slot], units)] = piece
                return carry

            return lax.fori_loop(0, filled_ref[g], copy, carry)

        lax.fori_loop(0, senders, sender, 0)

    vmem = pl.BlockSpec(memory_space=pltpu.VMEM)
    return pl.pallas_call(
        body,
        in_specs=[smem()] * 5 + [vmem] * 4 + unread(after),
        out_specs=vmem,
        out_shape=jax.ShapeDtypeStruct((room, UNIT, breadth), BF16),
        scratch_shapes=[
            pltpu.VMEM((edge, breadth), F32),
            pltpu.VMEM((sums.shape[0], UNIT, breadth), BF16),
        ],
        compiler_params=pltpu.CompilerParams(vmem_limit_bytes=GRANT),
        name="couple",
    )(ids, begins, filled, spots, shared, sums, others, high, low, *after)


def apply(turned, answers, begun, starts, used, part, cz, per_atom, after):
    cells, nodes, rows = turned.shape
    breadth = answers.shape[2]
    per_cell = rows // per_atom
    units = per_atom // UNIT
    side = begun.shape[2]
    deg = side - 1

    def body(starts_ref, used_ref, turned_ref, answers_ref, begun_ref, *refs):
        total_ref, stack_ref = refs[len(after) :]
        c = pl.program_id(0)

        @pl.when(c == 0)
        def _():
            total_ref[...] = begun_ref[...]

        row = lax.broadcasted_iota(jnp.int32, (per_atom, breadth), 0)
        for k in range(per_cell):
            entry = c * per_cell + k
            piece = answers_ref[pl.ds(starts_ref[entry], units)].astype(F32)
            piece = piece.reshape(per_atom, breadth)
            piece = jnp.where(row < used_ref[entry] * UNIT, piece, 0.0)
            stack_ref[k * per_atom : (k + 1) * per_atom] = piece.astype(BF16)
        result = jnp.dot(turned_ref[0], stack_ref[...], preferred_element_type=F32)
        u = pl.ds(c // cz * deg, side)
        w = pl.ds(c % cz * deg, side)
        total_ref[u, w] = total_ref[u, w] + result.reshape(side, side, side, breadth)

    shape = begun.shape[:3] + (breadth,)
    return pl.pallas_call(
        body,
        grid=(cells,),
        in_specs=[
            smem(),
            smem(),
            pl.BlockSpec((1, nodes, rows), lambda c: (c, 0, 0)),
            whole(answers.shape),
            pl.BlockSpec(shape, lambda c: (0, 0, 0, part), pipeline_mode=pl.Buffered(1)),
        ]
        + unread(after),
        out_specs=whole(shape),
        out_shape=jax.ShapeDtypeStruct(shape, F32),
        scratch_shapes=[pltpu.VMEM((rows, breadth), BF16)],
        compiler_params=pltpu.CompilerParams(vmem_limit_bytes=GRANT),
        name="apply",
    )(starts, used, turned, answers, begun, *after)


def finish(total, sides, ends, scale, older):
    span_u, span_w, span_v, breadth = total.shape

    def body(scale_ref, total_ref, prev_v_ref, next_v_ref, prev_u_ref, next_u_ref, *refs):
        out_ref = refs[-1]
        times = scale_ref[0]
        at = lax.broadcasted_iota(jnp.int32, (span_w, span_v, breadth), 1)

        def row(u, carry):
            first = prev_v_ref[u].astype(F32)[:, None]
            last = next_v_ref[u].astype(F32)[:, None]
            value = total_ref[u] + jnp.where(at == 0, first, 0.0)
            value = times * (value + jnp.where(at == span_v - 1, last, 0.0))
            if older is not None:
                value = value - refs[0][u]
            out_ref[u] = value
            return carry

        lax.fori_loop(0, span_u, row, 0)
        out_ref[0] = out_ref[0] + times * prev_u_ref[...].astype(F32)
        out_ref[span_u - 1] = out_ref[span_u - 1] + times * next_u_ref[...].astype(F32)

    vmem = pl.BlockSpec(memory_space=pltpu.VMEM)
    known = [] if older is None else [older]
    return pl.pallas_call(
        body,
        in_specs=[smem()] + [vmem] * (5 + len(known)),
        out_specs=vmem,
        out_shape=jax.ShapeDtypeStruct(total.shape, F32),
        compiler_params=pltpu.CompilerParams(vmem_limit_bytes=GRANT),
        name="finish",
    )(scale, total, *sides, *ends, *known)


def completed(total, scale, older):
    low_v = total[:, :, 0].astype(BF16)
    high_v = total[:, :, -1].astype(BF16)
    next_v = shifted(low_v, ("gy",), (-1,))
    prev_v = shifted(high_v, ("gy",), (1,))

    def edge(u):
        row = total[u]
        first = row[:, :1] + prev_v[u][:, None].astype(F32)
        last = row[:, -1:] + next_v[u][:, None].astype(F32)
        return jnp.concatenate([first, row[:, 1:-1], last], axis=1).astype(BF16)

    next_u = shifted(edge(0), ("gx",), (-1,))
    prev_u = shifted(edge(-1), ("gx",), (1,))
    return finish(total, (prev_v, next_v), (prev_u, next_u), scale, older)


def on_device(orbitals, cell_matrices, cell_nodes, projectors, entry_atom, coupling, proj_counts):
    span_x, span_y, layers, _ = orbitals.shape
    matrices = cell_matrices[0, 0]
    node_map = cell_nodes[0, 0]
    cells, per_cell, per_atom, nodes = projectors.shape[2:]
    shapes = projectors[0, 0].reshape(cells, per_cell * per_atom, nodes)
    atom_names = entry_atom[0, 0]
    side = round(nodes ** (1 / 3))
    deg = side - 1
    cz = (layers - 1) // deg
    assert span_y == deg and side**3 == nodes and cells * deg == span_x * cz
    entries = cells * per_cell
    n_gx, n_gy = lax.axis_size("gx"), lax.axis_size("gy")
    devices = n_gx * n_gy
    half = n_gy // 2
    senders = devices // 2
    home_atoms = coupling.shape[0]
    atoms = 2 * home_atoms
    each = 2 * max(2, 2 * entries // devices)
    slots = senders * each
    both = ("gx", "gy")
    teams = [
        [p * n_gy + h * half + r for p in range(n_gx) for r in range(half)] for h in range(2)
    ]

    def exchange(x):
        return lax.all_to_all(
            x, both, split_axis=0, concat_axis=0, axis_index_groups=teams, tiled=True
        )

    units = per_atom // UNIT
    my_x, my_y = lax.axis_index("gx"), lax.axis_index("gy")
    my_half, my_place = my_y // half, my_y % half
    me = my_x * n_gy + my_y
    mine = my_x * half + my_place

    notes = jnp.concatenate([atom_names.reshape(entries), proj_counts])
    notes = jnp.broadcast_to(notes, (devices, entries + home_atoms))
    notes = lax.all_to_all(notes, both, split_axis=0, concat_axis=0, tiled=True)
    names, counts = notes[:, :entries], notes[:, entries:]
    needs = (counts + UNIT - 1) // UNIT
    homes, inner = names // home_atoms, names % home_atoms
    homes_y = homes % n_gy
    at_home = (homes[:, :, None] == jnp.arange(devices)).astype(BF16)
    at_inner = (inner[:, :, None] == jnp.arange(home_atoms)).astype(BF16)
    picked = jnp.einsum("seh,hi->sei", at_home, needs.astype(BF16), preferred_element_type=F32)
    sizes = jnp.sum(picked * at_inner.astype(F32), axis=2).astype(jnp.int32)

    def by_half(x):
        return x.reshape((n_gx, 2, half) + x.shape[1:])

    split = [
        jnp.einsum(
            "seh,sei->hi",
            by_half(at_home)[:, h].reshape((senders,) + at_home.shape[1:]),
            by_half(at_inner)[:, h].reshape((senders,) + at_inner.shape[1:]),
            preferred_element_type=F32,
        )
        for h in range(2)
    ]
    common = ((split[0] > 0) & (split[1] > 0)).astype(jnp.int32)

    order = jnp.arange(entries)[None, :, None]
    present = homes[:, :, None] == jnp.arange(devices)
    sized = sizes[:, :, None]
    loads = jnp.sum(jnp.where(present, sized, 0), axis=1)
    ends = jnp.max(jnp.where(present, order * (2 * units) + sized, 0), axis=1)
    crossing = jnp.sum(common * needs, axis=1)
    table = jnp.concatenate([loads, ends, crossing[None]], axis=0).astype(F32)
    table = table.reshape(2 * devices + 1, n_gx, 2, half)
    lower = table[:, :, 0].reshape(-1, 1, senders)
    turned_to = np.zeros((senders, TURNS * TURNS, senders), np.float32)
    for j, k, p, r in itertools.product(range(TURNS), range(TURNS), range(n_gx), range(half)):
        source = (p + j) % n_gx * half + (r + k) % half
        turned_to[source, j * TURNS + k, p * half + r] = 1.0
    upper = jnp.einsum(
        "ah,hcg->acg",
        table[:, :, 1].reshape(-1, senders),
        jnp.asarray(turned_to),
        precision=lax.Precision.HIGHEST,
    )
    tail = jnp.maximum(lower, upper)[devices : 2 * devices].astype(jnp.int32) % (2 * units)
    joint = (lower + upper).astype(jnp.int32)
    cap = TIGHT * each * units // 64
    span = NARROW * atoms * units // 256
    fullest = jnp.max(joint[:devices] - tail + units, axis=(0, 2))
    widest = jnp.max(joint[-1] + units, axis=1)
    scores = jnp.maximum(fullest * span, widest * cap)
    best = jnp.argmin(scores).astype(jnp.int32)
    fits = jnp.min(scores) <= cap * span
    turn_x, turn_y = best // TURNS, best % TURNS
    over = homes_y // half
    held = over * home_atoms + inner
    places_x = (homes // n_gy - turn_x * over) % n_gx
    places_y = (homes_y % half - turn_y * over) % half
    collectors = places_x * half + places_y

    def of_me(x):
        return lax.dynamic_index_in_dim(x, me, 0, keepdims=False)

    def of_my_half(x):
        x = lax.dynamic_index_in_dim(by_half(x), my_half, 1, keepdims=False)
        return x.reshape((senders,) + x.shape[2:])

    def hosted(x):
        first = my_x * n_gy + my_place
        second = (my_x + turn_x) % n_gx * n_gy + half + (my_place + turn_y) % half
        rows = [lax.dynamic_index_in_dim(x, at, 0, keepdims=False) for at in (first, second)]
        return jnp.concatenate(rows)

    before = jnp.arange(entries)[:, None] < jnp.arange(entries)[None, :]
    own, used = of_me(collectors), of_me(sizes)
    ahead = before & (own[:, None] == own[None, :])
    offsets = jnp.sum(jnp.where(ahead, used[:, None], 0), axis=0)
    theirs = (of_my_half(collectors) == mine).astype(BF16)
    earlier = before.astype(BF16)
    ranks = jnp.dot(theirs, earlier, preferred_element_type=F32).astype(jnp.int32)
    lengths = theirs * of_my_half(sizes).astype(BF16)
    shifts = jnp.dot(lengths, earlier, preferred_element_type=F32).astype(jnp.int32)
    chosen = (ranks[:, None, :] == jnp.arange(each)[:, None]) & (theirs[:, None, :] > 0)
    ids = jnp.sum(jnp.where(chosen, of_my_half(held)[:, None, :], 0), axis=2).reshape(slots)
    places_in = jnp.sum(jnp.where(chosen, shifts[:, None, :], 0), axis=2)
    filled = jnp.sum(theirs.astype(F32), axis=1).astype(jnp.int32)
    shared = hosted(common)
    moved = shared * hosted(needs)
    upto = jnp.arange(atoms)[:, None] < jnp.arange(atoms)[None, :]
    spots = jnp.sum(jnp.where(upto, moved[:, None], 0), axis=0)

    flat = coupling.reshape(-1, 128)
    partner = shifted(flat, ("gy",), (half,))
    lower_mix = jnp.where(my_half > 0, partner, flat)
    upper_mix = jnp.where(my_half > 0, flat, partner)
    choices = [upper_mix] + [shifted(upper_mix, ("gx",), (-j,)) for j in range(1, TURNS)]
    upper_mix = lax.select_n(turn_x, *choices)
    choices = [upper_mix]
    for k in range(1, TURNS):
        pairs = [(h * half + (r + k) % half, h * half + r) for h in range(2) for r in range(half)]
        choices.append(lax.ppermute(upper_mix, "gy", pairs))
    upper_mix = lax.select_n(turn_y, *choices)
    mixers = jnp.concatenate([lower_mix, upper_mix], axis=0).reshape(atoms, per_atom, per_atom)
    active = (jnp.arange(per_atom)[None, :] < hosted(counts)[:, None]).astype(F32)
    mixers = mixers * active[:, :, None] * active[:, None, :]

    cell_ids = jnp.arange(cells, dtype=jnp.int32)[:, None]
    node_w = node_map % layers - cell_ids % cz * deg
    node_v = node_map // layers % (span_y + 1)
    node_u = node_map // (layers * (span_y + 1)) - cell_ids // cz * deg
    places = (node_u * side + node_w) * side + node_v
    places = places.reshape(cells, 1, nodes)

    row_next = shifted(orbitals[:1], ("gx",), (-1,))
    column_next = shifted(orbitals[:, :1], ("gy",), (-1,))
    corner_next = shifted(orbitals[:1, :1], both, (-1, -1))
    widened = jnp.concatenate(
        [
            jnp.concatenate([orbitals, column_next], axis=1),
            jnp.concatenate([row_next, corner_next], axis=1),
        ],
        axis=0,
    )
    grid = jnp.transpose(widened, (0, 2, 1, 3)).astype(F32)
    extended = grid.shape[:3]

    def advance(field, older, scale, known, cap, span):
        room = senders * cap
        starts = own * cap + offsets
        begins = (places_in + jnp.arange(senders)[:, None] * cap).reshape(slots)
        tables = (ids, begins, filled, spots, shared)
        if known is None:
            straight, local, *outgoing = project(field, shapes, starts, room, cz, per_atom, places)
        else:
            straight, stiff, turned, *mixing = known
            local, *outgoing = project(field, straight, starts, room, cz, per_atom)
        if known is None:
            stiff, turned = canonical(places, matrices, shapes, (local,))
            mixing = spread(mixers, (turned,))
        image = stiffen(stiff, local, extended, cz)
        after = ()
        gathered = []
        for packet in outgoing:
            incoming = exchange(packet)
            gathered.append(merge(incoming, tables, atoms, units, span, after))
            after = (gathered[-1][0],)
        after = after + (image,)
        answers = []
        for sums, sent in gathered:
            others = shifted(sent, ("gy",), (half,))
            replies = couple(sums, others, *mixing, tables, units, room, after)
            answers.append(exchange(replies))
            after = (replies,)
        totals = []
        for part in range(PARTS):
            totals.append(
                apply(turned, answers[part], image, starts, used, part, cz, per_atom, after)
            )
            after = (totals[-1],)
        total = jnp.concatenate(totals, axis=-1) if PARTS > 1 else totals[0]
        return completed(total, scale, older), (straight, stiff, turned, *mixing)

    def packed():
        known = None
        older, field = None, grid
        for step in range(FILTER_DEGREE):
            scale = jnp.full((1,), 1.0 if step == 0 else 2.0, F32)
            image, known = advance(field, older, scale, known, cap, span)
            older, field = field, image
        return field[:span_x, :, :span_y].astype(BF16)

    def roomy():
        def step(at, fields):
            older, field = fields
            scale = jnp.where(at == 0, 1.0, 2.0).astype(F32).reshape(1)
            image, _ = advance(
                field, older, scale, None, (each + 1) * units, (atoms + 1) * units
            )
            return field, image

        fields = (jnp.zeros_like(grid), grid)
        field = lax.fori_loop(0, FILTER_DEGREE, step, fields)[1]
        return field[:span_x, :, :span_y].astype(BF16)

    if MODE == "cond":
        filtered = lax.cond(fits, packed, roomy)
    else:
        filtered = packed() if MODE == "fast" else roomy()
    return jnp.transpose(filtered, (0, 2, 1, 3))


def solution(mesh):
    in_specs = (
        P("gx", "gy", None, None),
        P("gx", "gy", None, None, None),
        P("gx", "gy", None, None),
        P("gx", "gy", None, None, None, None),
        P("gx", "gy", None, None),
        P(("gx", "gy"), None, None),
        P(("gx", "gy")),
    )
    out_specs = P("gx", "gy", None, None)
    return jax.shard_map(
        on_device, mesh=mesh, in_specs=in_specs, out_specs=out_specs, check_vma=False
    )
```

```python
import itertools

import jax
import jax.numpy as jnp
import numpy as np
from jax import lax
from jax.experimental import pallas as pl
from jax.experimental.pallas import tpu as pltpu
from jax.sharding import PartitionSpec as P


FILTER_DEGREE = 3
PARTS = 1
UNIT = 8
TIGHT = 46
NARROW = 172
TURNS = 4
MODE = "cond"
GRANT = 20 * 1024 * 1024
GROUP = 8
BF16 = jnp.bfloat16
F32 = jnp.float32


def shifted(x, axes, by):
    sizes = [lax.axis_size(a) for a in axes]
    pairs = []
    for place in itertools.product(*[range(s) for s in sizes]):
        source = 0
        target = 0
        for at, step, size in zip(place, by, sizes):
            source = source * size + at
            target = target * size + (at + step) % size
        pairs.append((source, target))
    return lax.ppermute(x, axes if len(axes) > 1 else axes[0], pairs)


def whole(shape):
    return pl.BlockSpec(shape, lambda c: (0,) * len(shape), pipeline_mode=pl.Buffered(1))


def smem():
    return pl.BlockSpec(memory_space=pltpu.SMEM)


def unread(after):
    return [pl.BlockSpec(memory_space=pl.ANY)] * len(after)


def pick_matrix(place_ref, nodes):
    spots = lax.broadcasted_iota(jnp.int32, (nodes, nodes), 0)
    return (spots == place_ref[0]).astype(BF16)


LAST = (((1,), (1,)), ((), ()))


def canonical(places, matrices, shapes, after):
    cells, rows, nodes = shapes.shape

    def body(place_ref, matrix_ref, shape_ref, *refs):
        stiff_ref, turned_ref = refs[len(after) :]
        pick = pick_matrix(place_ref, nodes)
        half = jnp.dot(pick, matrix_ref[0], preferred_element_type=F32).astype(BF16)
        full = lax.dot_general(half, pick, LAST, preferred_element_type=F32)
        stiff_ref[0] = full.astype(BF16)
        flipped = lax.dot_general(pick, shape_ref[0], LAST, preferred_element_type=F32)
        turned_ref[0] = flipped.astype(BF16)

    def block(shape):
        return pl.BlockSpec((1,) + shape, lambda c: (c, 0, 0))

    return pl.pallas_call(
        body,
        grid=(cells,),
        in_specs=[block((1, nodes)), block((nodes, nodes)), block((rows, nodes))] + unread(after),
        out_specs=[block((nodes, nodes)), block((nodes, rows))],
        out_shape=[
            jax.ShapeDtypeStruct((cells, nodes, nodes), BF16),
            jax.ShapeDtypeStruct((cells, nodes, rows), BF16),
        ],
        compiler_params=pltpu.CompilerParams(vmem_limit_bytes=GRANT),
        name="canonical",
    )(places, matrices, shapes, *after)


def spread(mixers, after):
    atoms, per_atom, _ = mixers.shape
    groups = atoms // GROUP
    edge = GROUP * per_atom

    def body(mixers_ref, *refs):
        high_ref, low_ref = refs[len(after) :]
        rows = lax.broadcasted_iota(jnp.int32, (edge, edge), 0) // per_atom
        columns = lax.broadcasted_iota(jnp.int32, (edge, edge), 1) // per_atom

        def one(g, carry):
            block = mixers_ref[pl.ds(g * GROUP, GROUP)].reshape(edge, per_atom)
            block = jnp.concatenate([block] * GROUP, axis=1)
            block = jnp.where(rows == columns, block, 0.0)
            high = block.astype(BF16)
            high_ref[g] = high
            low_ref[g] = (block - high.astype(F32)).astype(BF16)
            return carry

        lax.fori_loop(0, groups, one, 0)

    vmem = pl.BlockSpec(memory_space=pltpu.VMEM)
    return pl.pallas_call(
        body,
        in_specs=[vmem] + unread(after),
        out_specs=[vmem, vmem],
        out_shape=[jax.ShapeDtypeStruct((groups, edge, edge), BF16)] * 2,
        compiler_params=pltpu.CompilerParams(vmem_limit_bytes=GRANT),
        name="spread",
    )(mixers, *after)


def project(field, straight, starts, room, cz, per_atom, places=None):
    cells, rows, nodes = straight.shape
    side = field.shape[2]
    deg = side - 1
    breadth = field.shape[3]
    per_cell = rows // per_atom
    width = breadth // PARTS
    units = per_atom // UNIT
    raw = places is not None

    def body(starts_ref, field_ref, straight_ref, *refs):
        if raw:
            place_ref, grid_ref, *refs = refs
        local_ref, *out_refs = refs
        c = pl.program_id(0)
        u = c // cz * deg
        w = c % cz * deg
        block = field_ref[pl.ds(u, side), pl.ds(w, side)]
        local = block.reshape(nodes, breadth).astype(BF16)
        local_ref[0] = local
        rows_of = straight_ref[0]
        if raw:
            pick = pick_matrix(place_ref, nodes)
            rows_of = lax.dot_general(rows_of, pick, LAST, preferred_element_type=F32)
            rows_of = rows_of.astype(BF16)
            grid_ref[0] = rows_of
        values = jnp.dot(rows_of, local, preferred_element_type=F32)
        for k in range(per_cell):
            start = starts_ref[c * per_cell + k]
            for s, out_ref in enumerate(out_refs):
                piece = values[k * per_atom : (k + 1) * per_atom, s * width : (s + 1) * width]
                out_ref[pl.ds(start, units)] = piece.reshape(units, UNIT, width).astype(BF16)

    def block(shape):
        return pl.BlockSpec((1,) + shape, lambda c: (c, 0, 0))

    turning = [jax.ShapeDtypeStruct(straight.shape, BF16)] if raw else []
    return pl.pallas_call(
        body,
        grid=(cells,),
        in_specs=[smem(), whole(field.shape), block((rows, nodes))]
        + ([block((1, nodes))] if raw else []),
        out_specs=([block((rows, nodes))] if raw else [])
        + [block((nodes, breadth))]
        + [whole((room, UNIT, width))] * PARTS,
        out_shape=turning
        + [jax.ShapeDtypeStruct((cells, nodes, breadth), BF16)]
        + [jax.ShapeDtypeStruct((room, UNIT, width), BF16)] * PARTS,
        compiler_params=pltpu.CompilerParams(vmem_limit_bytes=GRANT),
        name="project",
    )(starts, field, straight, *([places] if raw else []))


def stiffen(stiff, local, extended, cz):
    cells, nodes, _ = stiff.shape
    breadth = local.shape[2]
    side = extended[2]
    deg = side - 1

    def body(stiff_ref, local_ref, total_ref):
        c = pl.program_id(0)

        @pl.when(c == 0)
        def _():
            total_ref[...] = jnp.zeros_like(total_ref)

        result = jnp.dot(stiff_ref[0], local_ref[0], preferred_element_type=F32)
        u = pl.ds(c // cz * deg, side)
        w = pl.ds(c % cz * deg, side)
        total_ref[u, w] = total_ref[u, w] + result.reshape(side, side, side, breadth)

    shape = extended + (breadth,)
    return pl.pallas_call(
        body,
        grid=(cells,),
        in_specs=[
            pl.BlockSpec((1, nodes, nodes), lambda c: (c, 0, 0)),
            pl.BlockSpec((1, nodes, breadth), lambda c: (c, 0, 0)),
        ],
        out_specs=whole(shape),
        out_shape=jax.ShapeDtypeStruct(shape, F32),
        compiler_params=pltpu.CompilerParams(vmem_limit_bytes=GRANT),
        name="stiffen",
    )(stiff, local)


def merge(incoming, tables, atoms, units, span, after):
    breadth = incoming.shape[2]
    ids, begins, filled, spots, _ = tables
    senders = filled.shape[0]
    each = ids.shape[0] // senders

    def body(ids_ref, begins_ref, filled_ref, spots_ref, incoming_ref, *refs):
        sums_ref, sent_ref = refs[len(after) :]
        sums_ref[...] = jnp.zeros_like(sums_ref)

        def sender(g, carry):
            def add(j, carry):
                slot = g * each + j
                into = pl.ds(ids_ref[slot] * units, units)
                piece = incoming_ref[pl.ds(begins_ref[slot], units)].astype(F32)
                sums_ref[into] = sums_ref[into] + piece
                return carry

            return lax.fori_loop(0, filled_ref[g], add, carry)

        lax.fori_loop(0, senders, sender, 0)

        def pack(a, carry):
            piece = sums_ref[pl.ds(a * units, units)]
            sent_ref[pl.ds(spots_ref[a], units)] = piece.astype(BF16)
            return carry

        lax.fori_loop(0, atoms, pack, 0, unroll=4)

    return pl.pallas_call(
        body,
        in_specs=[smem()] * 4 + [pl.BlockSpec(memory_space=pltpu.VMEM)] + unread(after),
        out_specs=[pl.BlockSpec(memory_space=pltpu.VMEM)] * 2,
        out_shape=[
            jax.ShapeDtypeStruct((atoms * units, UNIT, breadth), F32),
            jax.ShapeDtypeStruct((span, UNIT, breadth), BF16),
        ],
        compiler_params=pltpu.CompilerParams(vmem_limit_bytes=GRANT),
        name="merge",
    )(ids, begins, filled, spots, incoming, *after)


def couple(sums, others, high, low, tables, units, room, after):
    breadth = sums.shape[2]
    groups, edge, _ = high.shape
    ids, begins, filled, spots, shared = tables
    senders = filled.shape[0]
    each = ids.shape[0] // senders
    rows = units * UNIT

    def body(ids_ref, begins_ref, filled_ref, spots_ref, shared_ref, sums_ref, others_ref, *refs):
        high_ref, low_ref = refs[:2]
        out_ref, total_ref, kept_ref = refs[2 + len(after) :]

        def mix(g, carry):
            for m in range(GROUP):
                a = g * GROUP + m
                piece = others_ref[pl.ds(spots_ref[a], units)].astype(F32)
                piece = jnp.where(shared_ref[a] > 0, piece, 0.0)
                piece = sums_ref[pl.ds(a * units, units)] + piece
                total_ref[m * rows : (m + 1) * rows] = piece.reshape(rows, breadth)
            total = total_ref[...]
            upper = total.astype(BF16)
            lower = (total - upper.astype(F32)).astype(BF16)
            mixed = jnp.dot(high_ref[g], upper, preferred_element_type=F32)
            mixed = mixed + jnp.dot(low_ref[g], upper, preferred_element_type=F32)
            mixed = mixed + jnp.dot(high_ref[g], lower, preferred_element_type=F32)
            mixed = mixed.reshape(GROUP * units, UNIT, breadth).astype(BF16)
            kept_ref[pl.ds(g * GROUP * units, GROUP * units)] = mixed
            return carry

        lax.fori_loop(0, groups, mix, 0, unroll=2)

        def sender(g, carry):
            def copy(j, carry):
                slot = g * each + j
                piece = kept_ref[pl.ds(ids_ref[slot] * units, units)]
                out_ref[pl.ds(begins_ref[slot], units)] = piece
                return carry

            return lax.fori_loop(0, filled_ref[g], copy, carry)

        lax.fori_loop(0, senders, sender, 0)

    vmem = pl.BlockSpec(memory_space=pltpu.VMEM)
    return pl.pallas_call(
        body,
        in_specs=[smem()] * 5 + [vmem] * 4 + unread(after),
        out_specs=vmem,
        out_shape=jax.ShapeDtypeStruct((room, UNIT, breadth), BF16),
        scratch_shapes=[
            pltpu.VMEM((edge, breadth), F32),
            pltpu.VMEM((sums.shape[0], UNIT, breadth), BF16),
        ],
        compiler_params=pltpu.CompilerParams(vmem_limit_bytes=GRANT),
        name="couple",
    )(ids, begins, filled, spots, shared, sums, others, high, low, *after)


def apply(turned, answers, begun, starts, used, part, cz, per_atom, after):
    cells, nodes, rows = turned.shape
    breadth = answers.shape[2]
    per_cell = rows // per_atom
    units = per_atom // UNIT
    side = begun.shape[2]
    deg = side - 1

    def body(starts_ref, used_ref, turned_ref, answers_ref, begun_ref, *refs):
        total_ref, stack_ref = refs[len(after) :]
        c = pl.program_id(0)

        @pl.when(c == 0)
        def _():
            total_ref[...] = begun_ref[...]

        row = lax.broadcasted_iota(jnp.int32, (per_atom, breadth), 0)
        for k in range(per_cell):
            entry = c * per_cell + k
            piece = answers_ref[pl.ds(starts_ref[entry], units)].astype(F32)
            piece = piece.reshape(per_atom, breadth)
            piece = jnp.where(row < used_ref[entry] * UNIT, piece, 0.0)
            stack_ref[k * per_atom : (k + 1) * per_atom] = piece.astype(BF16)
        result = jnp.dot(turned_ref[0], stack_ref[...], preferred_element_type=F32)
        u = pl.ds(c // cz * deg, side)
        w = pl.ds(c % cz * deg, side)
        total_ref[u, w] = total_ref[u, w] + result.reshape(side, side, side, breadth)

    shape = begun.shape[:3] + (breadth,)
    return pl.pallas_call(
        body,
        grid=(cells,),
        in_specs=[
            smem(),
            smem(),
            pl.BlockSpec((1, nodes, rows), lambda c: (c, 0, 0)),
            whole(answers.shape),
            pl.BlockSpec(shape, lambda c: (0, 0, 0, part), pipeline_mode=pl.Buffered(1)),
        ]
        + unread(after),
        out_specs=whole(shape),
        out_shape=jax.ShapeDtypeStruct(shape, F32),
        scratch_shapes=[pltpu.VMEM((rows, breadth), BF16)],
        compiler_params=pltpu.CompilerParams(vmem_limit_bytes=GRANT),
        name="apply",
    )(starts, used, turned, answers, begun, *after)


def finish(total, sides, ends, scale, older):
    span_u, span_w, span_v, breadth = total.shape

    def body(scale_ref, total_ref, prev_v_ref, next_v_ref, prev_u_ref, next_u_ref, *refs):
        out_ref = refs[-1]
        times = scale_ref[0]
        at = lax.broadcasted_iota(jnp.int32, (span_w, span_v, breadth), 1)

        def row(u, carry):
            first = prev_v_ref[u].astype(F32)[:, None]
            last = next_v_ref[u].astype(F32)[:, None]
            value = total_ref[u] + jnp.where(at == 0, first, 0.0)
            value = times * (value + jnp.where(at == span_v - 1, last, 0.0))
            if older is not None:
                value = value - refs[0][u]
            out_ref[u] = value
            return carry

        lax.fori_loop(0, span_u, row, 0)
        out_ref[0] = out_ref[0] + times * prev_u_ref[...].astype(F32)
        out_ref[span_u - 1] = out_ref[span_u - 1] + times * next_u_ref[...].astype(F32)

    vmem = pl.BlockSpec(memory_space=pltpu.VMEM)
    known = [] if older is None else [older]
    return pl.pallas_call(
        body,
        in_specs=[smem()] + [vmem] * (5 + len(known)),
        out_specs=vmem,
        out_shape=jax.ShapeDtypeStruct(total.shape, F32),
        compiler_params=pltpu.CompilerParams(vmem_limit_bytes=GRANT),
        name="finish",
    )(scale, total, *sides, *ends, *known)


def completed(total, scale, older):
    low_v = total[:, :, 0].astype(BF16)
    high_v = total[:, :, -1].astype(BF16)
    next_v = shifted(low_v, ("gy",), (-1,))
    prev_v = shifted(high_v, ("gy",), (1,))

    def edge(u):
        row = total[u]
        first = row[:, :1] + prev_v[u][:, None].astype(F32)
        last = row[:, -1:] + next_v[u][:, None].astype(F32)
        return jnp.concatenate([first, row[:, 1:-1], last], axis=1).astype(BF16)

    next_u = shifted(edge(0), ("gx",), (-1,))
    prev_u = shifted(edge(-1), ("gx",), (1,))
    return finish(total, (prev_v, next_v), (prev_u, next_u), scale, older)


def on_device(orbitals, cell_matrices, cell_nodes, projectors, entry_atom, coupling, proj_counts):
    span_x, span_y, layers, _ = orbitals.shape
    matrices = cell_matrices[0, 0]
    node_map = cell_nodes[0, 0]
    cells, per_cell, per_atom, nodes = projectors.shape[2:]
    shapes = projectors[0, 0].reshape(cells, per_cell * per_atom, nodes)
    atom_names = entry_atom[0, 0]
    side = round(nodes ** (1 / 3))
    deg = side - 1
    cz = (layers - 1) // deg
    assert span_y == deg and side**3 == nodes and cells * deg == span_x * cz
    entries = cells * per_cell
    n_gx, n_gy = lax.axis_size("gx"), lax.axis_size("gy")
    devices = n_gx * n_gy
    half = n_gy // 2
    senders = devices // 2
    home_atoms = coupling.shape[0]
    atoms = 2 * home_atoms
    each = 2 * max(2, 2 * entries // devices)
    slots = senders * each
    both = ("gx", "gy")
    teams = [
        [p * n_gy + h * half + r for p in range(n_gx) for r in range(half)] for h in range(2)
    ]

    def exchange(x):
        return lax.all_to_all(
            x, both, split_axis=0, concat_axis=0, axis_index_groups=teams, tiled=True
        )

    units = per_atom // UNIT
    my_x, my_y = lax.axis_index("gx"), lax.axis_index("gy")
    my_half, my_place = my_y // half, my_y % half
    me = my_x * n_gy + my_y
    mine = my_x * half + my_place

    notes = jnp.concatenate([atom_names.reshape(entries), proj_counts])
    notes = jnp.broadcast_to(notes, (devices, entries + home_atoms))
    notes = lax.all_to_all(notes, both, split_axis=0, concat_axis=0, tiled=True)
    names, counts = notes[:, :entries], notes[:, entries:]
    needs = (counts + UNIT - 1) // UNIT
    homes, inner = names // home_atoms, names % home_atoms
    homes_y = homes % n_gy
    at_home = (homes[:, :, None] == jnp.arange(devices)).astype(BF16)
    at_inner = (inner[:, :, None] == jnp.arange(home_atoms)).astype(BF16)
    picked = jnp.einsum("seh,hi->sei", at_home, needs.astype(BF16), preferred_element_type=F32)
    sizes = jnp.sum(picked * at_inner.astype(F32), axis=2).astype(jnp.int32)

    def by_half(x):
        return x.reshape((n_gx, 2, half) + x.shape[1:])

    split = [
        jnp.einsum(
            "seh,sei->hi",
            by_half(at_home)[:, h].reshape((senders,) + at_home.shape[1:]),
            by_half(at_inner)[:, h].reshape((senders,) + at_inner.shape[1:]),
            preferred_element_type=F32,
        )
        for h in range(2)
    ]
    common = ((split[0] > 0) & (split[1] > 0)).astype(jnp.int32)

    order = jnp.arange(entries)[None, :, None]
    present = homes[:, :, None] == jnp.arange(devices)
    sized = sizes[:, :, None]
    loads = jnp.sum(jnp.where(present, sized, 0), axis=1)
    ends = jnp.max(jnp.where(present, order * (2 * units) + sized, 0), axis=1)
    crossing = jnp.sum(common * needs, axis=1)
    table = jnp.concatenate([loads, ends, crossing[None]], axis=0).astype(F32)
    table = table.reshape(2 * devices + 1, n_gx, 2, half)
    lower = table[:, :, 0].reshape(-1, 1, senders)
    turned_to = np.zeros((senders, TURNS * TURNS, senders), np.float32)
    for j, k, p, r in itertools.product(range(TURNS), range(TURNS), range(n_gx), range(half)):
        source = (p + j) % n_gx * half + (r + k) % half
        turned_to[source, j * TURNS + k, p * half + r] = 1.0
    upper = jnp.einsum(
        "ah,hcg->acg",
        table[:, :, 1].reshape(-1, senders),
        jnp.asarray(turned_to),
        precision=lax.Precision.HIGHEST,
    )
    tail = jnp.maximum(lower, upper)[devices : 2 * devices].astype(jnp.int32) % (2 * units)
    joint = (lower + upper).astype(jnp.int32)
    cap = TIGHT * each * units // 64
    span = NARROW * atoms * units // 256
    fullest = jnp.max(joint[:devices] - tail + units, axis=(0, 2))
    widest = jnp.max(joint[-1] + units, axis=1)
    scores = jnp.maximum(fullest * span, widest * cap)
    best = jnp.argmin(scores).astype(jnp.int32)
    fits = jnp.min(scores) <= cap * span
    turn_x, turn_y = best // TURNS, best % TURNS
    over = homes_y // half
    held = over * home_atoms + inner
    places_x = (homes // n_gy - turn_x * over) % n_gx
    places_y = (homes_y % half - turn_y * over) % half
    collectors = places_x * half + places_y

    def of_me(x):
        return lax.dynamic_index_in_dim(x, me, 0, keepdims=False)

    def of_my_half(x):
        x = lax.dynamic_index_in_dim(by_half(x), my_half, 1, keepdims=False)
        return x.reshape((senders,) + x.shape[2:])

    def hosted(x):
        first = my_x * n_gy + my_place
        second = (my_x + turn_x) % n_gx * n_gy + half + (my_place + turn_y) % half
        rows = [lax.dynamic_index_in_dim(x, at, 0, keepdims=False) for at in (first, second)]
        return jnp.concatenate(rows)

    before = jnp.arange(entries)[:, None] < jnp.arange(entries)[None, :]
    own, used = of_me(collectors), of_me(sizes)
    ahead = before & (own[:, None] == own[None, :])
    offsets = jnp.sum(jnp.where(ahead, used[:, None], 0), axis=0)
    theirs = (of_my_half(collectors) == mine).astype(BF16)
    earlier = before.astype(BF16)
    ranks = jnp.dot(theirs, earlier, preferred_element_type=F32).astype(jnp.int32)
    lengths = theirs * of_my_half(sizes).astype(BF16)
    shifts = jnp.dot(lengths, earlier, preferred_element_type=F32).astype(jnp.int32)
    chosen = (ranks[:, None, :] == jnp.arange(each)[:, None]) & (theirs[:, None, :] > 0)
    ids = jnp.sum(jnp.where(chosen, of_my_half(held)[:, None, :], 0), axis=2).reshape(slots)
    places_in = jnp.sum(jnp.where(chosen, shifts[:, None, :], 0), axis=2)
    filled = jnp.sum(theirs.astype(F32), axis=1).astype(jnp.int32)
    shared = hosted(common)
    moved = shared * hosted(needs)
    upto = jnp.arange(atoms)[:, None] < jnp.arange(atoms)[None, :]
    spots = jnp.sum(jnp.where(upto, moved[:, None], 0), axis=0)

    flat = coupling.reshape(-1, 128)
    partner = shifted(flat, ("gy",), (half,))
    lower_mix = jnp.where(my_half > 0, partner, flat)
    upper_mix = jnp.where(my_half > 0, flat, partner)
    choices = [upper_mix] + [shifted(upper_mix, ("gx",), (-j,)) for j in range(1, TURNS)]
    upper_mix = lax.select_n(turn_x, *choices)
    choices = [upper_mix]
    for k in range(1, TURNS):
        pairs = [(h * half + (r + k) % half, h * half + r) for h in range(2) for r in range(half)]
        choices.append(lax.ppermute(upper_mix, "gy", pairs))
    upper_mix = lax.select_n(turn_y, *choices)
    mixers = jnp.concatenate([lower_mix, upper_mix], axis=0).reshape(atoms, per_atom, per_atom)
    active = (jnp.arange(per_atom)[None, :] < hosted(counts)[:, None]).astype(F32)
    mixers = mixers * active[:, :, None] * active[:, None, :]

    cell_ids = jnp.arange(cells, dtype=jnp.int32)[:, None]
    node_w = node_map % layers - cell_ids % cz * deg
    node_v = node_map // layers % (span_y + 1)
    node_u = node_map // (layers * (span_y + 1)) - cell_ids // cz * deg
    places = (node_u * side + node_w) * side + node_v
    places = places.reshape(cells, 1, nodes)

    row_next = shifted(orbitals[0], ("gx",), (-1,))[None]
    column_next = shifted(orbitals[:, 0], ("gy",), (-1,))[:, None]
    corner_next = shifted(orbitals[0, 0], both, (-1, -1))[None, None]
    widened = jnp.concatenate(
        [
            jnp.concatenate([orbitals, column_next], axis=1),
            jnp.concatenate([row_next, corner_next], axis=1),
        ],
        axis=0,
    )
    grid = jnp.transpose(widened, (0, 2, 1, 3)).astype(F32)
    extended = grid.shape[:3]

    def advance(field, older, scale, known, cap, span):
        room = senders * cap
        starts = own * cap + offsets
        begins = (places_in + jnp.arange(senders)[:, None] * cap).reshape(slots)
        tables = (ids, begins, filled, spots, shared)
        if known is None:
            straight, local, *outgoing = project(field, shapes, starts, room, cz, per_atom, places)
        else:
            straight, stiff, turned, *mixing = known
            local, *outgoing = project(field, straight, starts, room, cz, per_atom)
        if known is None:
            stiff, turned = canonical(places, matrices, shapes, (local,))
            mixing = spread(mixers, (turned,))
        image = stiffen(stiff, local, extended, cz)
        after = ()
        gathered = []
        for packet in outgoing:
            incoming = exchange(packet)
            gathered.append(merge(incoming, tables, atoms, units, span, after))
            after = (gathered[-1][0],)
        after = after + (image,)
        answers = []
        for sums, sent in gathered:
            others = shifted(sent, ("gy",), (half,))
            replies = couple(sums, others, *mixing, tables, units, room, after)
            answers.append(exchange(replies))
            after = (replies,)
        totals = []
        for part in range(PARTS):
            totals.append(
                apply(turned, answers[part], image, starts, used, part, cz, per_atom, after)
            )
            after = (totals[-1],)
        total = jnp.concatenate(totals, axis=-1) if PARTS > 1 else totals[0]
        return completed(total, scale, older), (straight, stiff, turned, *mixing)

    def packed():
        known = None
        older, field = None, grid
        for step in range(FILTER_DEGREE):
            scale = jnp.full((1,), 1.0 if step == 0 else 2.0, F32)
            image, known = advance(field, older, scale, known, cap, span)
            older, field = field, image
        return field[:span_x, :, :span_y].astype(BF16)

    def roomy():
        def step(at, fields):
            older, field = fields
            scale = jnp.where(at == 0, 1.0, 2.0).astype(F32).reshape(1)
            image, _ = advance(
                field, older, scale, None, (each + 1) * units, (atoms + 1) * units
            )
            return field, image

        fields = (jnp.zeros_like(grid), grid)
        field = lax.fori_loop(0, FILTER_DEGREE, step, fields)[1]
        return field[:span_x, :, :span_y].astype(BF16)

    if MODE == "cond":
        filtered = lax.cond(fits, packed, roomy)
    else:
        filtered = packed() if MODE == "fast" else roomy()
    return jnp.transpose(filtered, (0, 2, 1, 3))


def solution(mesh):
    in_specs = (
        P("gx", "gy", None, None),
        P("gx", "gy", None, None, None),
        P("gx", "gy", None, None),
        P("gx", "gy", None, None, None, None),
        P("gx", "gy", None, None),
        P(("gx", "gy"), None, None),
        P(("gx", "gy")),
    )
    out_specs = P("gx", "gy", None, None)
    return jax.shard_map(
        on_device, mesh=mesh, in_specs=in_specs, out_specs=out_specs, check_vma=False
    )
```

```python
import itertools

import jax
import jax.numpy as jnp
import numpy as np
from jax import lax
from jax.experimental import pallas as pl
from jax.experimental.pallas import tpu as pltpu
from jax.sharding import PartitionSpec as P


FILTER_DEGREE = 3
PARTS = 1
UNIT = 8
TIGHT = 46
NARROW = 172
TURNS = 4
MODE = "cond"
GRANT = 20 * 1024 * 1024
GROUP = 8
BF16 = jnp.bfloat16
F32 = jnp.float32


def shifted(x, axes, by):
    sizes = [lax.axis_size(a) for a in axes]
    pairs = []
    for place in itertools.product(*[range(s) for s in sizes]):
        source = 0
        target = 0
        for at, step, size in zip(place, by, sizes):
            source = source * size + at
            target = target * size + (at + step) % size
        pairs.append((source, target))
    return lax.ppermute(x, axes if len(axes) > 1 else axes[0], pairs)


def whole(shape):
    return pl.BlockSpec(shape, lambda c: (0,) * len(shape), pipeline_mode=pl.Buffered(1))


def smem():
    return pl.BlockSpec(memory_space=pltpu.SMEM)


def unread(after):
    return [pl.BlockSpec(memory_space=pl.ANY)] * len(after)


def pick_matrix(place_ref, nodes):
    spots = lax.broadcasted_iota(jnp.int32, (nodes, nodes), 0)
    return (spots == place_ref[0]).astype(BF16)


LAST = (((1,), (1,)), ((), ()))


def canonical(places, matrices, shapes, after):
    cells, rows, nodes = shapes.shape

    def body(place_ref, matrix_ref, shape_ref, *refs):
        stiff_ref, turned_ref = refs[len(after) :]
        pick = pick_matrix(place_ref, nodes)
        half = jnp.dot(pick, matrix_ref[0], preferred_element_type=F32).astype(BF16)
        full = lax.dot_general(half, pick, LAST, preferred_element_type=F32)
        stiff_ref[0] = full.astype(BF16)
        flipped = lax.dot_general(pick, shape_ref[0], LAST, preferred_element_type=F32)
        turned_ref[0] = flipped.astype(BF16)

    def block(shape):
        return pl.BlockSpec((1,) + shape, lambda c: (c, 0, 0))

    return pl.pallas_call(
        body,
        grid=(cells,),
        in_specs=[block((1, nodes)), block((nodes, nodes)), block((rows, nodes))] + unread(after),
        out_specs=[block((nodes, nodes)), block((nodes, rows))],
        out_shape=[
            jax.ShapeDtypeStruct((cells, nodes, nodes), BF16),
            jax.ShapeDtypeStruct((cells, nodes, rows), BF16),
        ],
        compiler_params=pltpu.CompilerParams(vmem_limit_bytes=GRANT),
        name="canonical",
    )(places, matrices, shapes, *after)


def spread(mixers, after):
    atoms, per_atom, _ = mixers.shape
    groups = atoms // GROUP
    edge = GROUP * per_atom

    def body(mixers_ref, *refs):
        high_ref, low_ref = refs[len(after) :]
        rows = lax.broadcasted_iota(jnp.int32, (edge, edge), 0) // per_atom
        columns = lax.broadcasted_iota(jnp.int32, (edge, edge), 1) // per_atom

        def one(g, carry):
            block = mixers_ref[pl.ds(g * GROUP, GROUP)].reshape(edge, per_atom)
            block = jnp.concatenate([block] * GROUP, axis=1)
            block = jnp.where(rows == columns, block, 0.0)
            high = block.astype(BF16)
            high_ref[g] = high
            low_ref[g] = (block - high.astype(F32)).astype(BF16)
            return carry

        lax.fori_loop(0, groups, one, 0)

    vmem = pl.BlockSpec(memory_space=pltpu.VMEM)
    return pl.pallas_call(
        body,
        in_specs=[vmem] + unread(after),
        out_specs=[vmem, vmem],
        out_shape=[jax.ShapeDtypeStruct((groups, edge, edge), BF16)] * 2,
        compiler_params=pltpu.CompilerParams(vmem_limit_bytes=GRANT),
        name="spread",
    )(mixers, *after)


def project(field, straight, starts, room, cz, per_atom, places=None):
    cells, rows, nodes = straight.shape
    side = field.shape[2]
    deg = side - 1
    breadth = field.shape[3]
    per_cell = rows // per_atom
    width = breadth // PARTS
    units = per_atom // UNIT
    raw = places is not None

    def body(starts_ref, field_ref, straight_ref, *refs):
        if raw:
            place_ref, grid_ref, *refs = refs
        local_ref, *out_refs = refs
        c = pl.program_id(0)
        u = c // cz * deg
        w = c % cz * deg
        block = field_ref[pl.ds(u, side), pl.ds(w, side)]
        local = block.reshape(nodes, breadth).astype(BF16)
        local_ref[0] = local
        rows_of = straight_ref[0]
        if raw:
            pick = pick_matrix(place_ref, nodes)
            rows_of = lax.dot_general(rows_of, pick, LAST, preferred_element_type=F32)
            rows_of = rows_of.astype(BF16)
            grid_ref[0] = rows_of
        values = jnp.dot(rows_of, local, preferred_element_type=F32)
        for k in range(per_cell):
            start = starts_ref[c * per_cell + k]
            for s, out_ref in enumerate(out_refs):
                piece = values[k * per_atom : (k + 1) * per_atom, s * width : (s + 1) * width]
                out_ref[pl.ds(start, units)] = piece.reshape(units, UNIT, width).astype(BF16)

    def block(shape):
        return pl.BlockSpec((1,) + shape, lambda c: (c, 0, 0))

    turning = [jax.ShapeDtypeStruct(straight.shape, BF16)] if raw else []
    return pl.pallas_call(
        body,
        grid=(cells,),
        in_specs=[smem(), whole(field.shape), block((rows, nodes))]
        + ([block((1, nodes))] if raw else []),
        out_specs=([block((rows, nodes))] if raw else [])
        + [block((nodes, breadth))]
        + [whole((room, UNIT, width))] * PARTS,
        out_shape=turning
        + [jax.ShapeDtypeStruct((cells, nodes, breadth), BF16)]
        + [jax.ShapeDtypeStruct((room, UNIT, width), BF16)] * PARTS,
        compiler_params=pltpu.CompilerParams(vmem_limit_bytes=GRANT),
        name="project",
    )(starts, field, straight, *([places] if raw else []))


def stiffen(stiff, local, extended, cz):
    cells, nodes, _ = stiff.shape
    breadth = local.shape[2]
    side = extended[2]
    deg = side - 1

    def body(stiff_ref, local_ref, total_ref):
        c = pl.program_id(0)

        @pl.when(c == 0)
        def _():
            total_ref[...] = jnp.zeros_like(total_ref)

        result = jnp.dot(stiff_ref[0], local_ref[0], preferred_element_type=F32)
        u = pl.ds(c // cz * deg, side)
        w = pl.ds(c % cz * deg, side)
        total_ref[u, w] = total_ref[u, w] + result.reshape(side, side, side, breadth)

    shape = extended + (breadth,)
    return pl.pallas_call(
        body,
        grid=(cells,),
        in_specs=[
            pl.BlockSpec((1, nodes, nodes), lambda c: (c, 0, 0)),
            pl.BlockSpec((1, nodes, breadth), lambda c: (c, 0, 0)),
        ],
        out_specs=whole(shape),
        out_shape=jax.ShapeDtypeStruct(shape, F32),
        compiler_params=pltpu.CompilerParams(vmem_limit_bytes=GRANT),
        name="stiffen",
    )(stiff, local)


def merge(incoming, tables, atoms, units, span, after):
    breadth = incoming.shape[2]
    ids, begins, filled, spots, _ = tables
    senders = filled.shape[0]
    each = ids.shape[0] // senders

    def body(ids_ref, begins_ref, filled_ref, spots_ref, incoming_ref, *refs):
        sums_ref, sent_ref = refs[len(after) :]
        sums_ref[...] = jnp.zeros_like(sums_ref)

        def sender(g, carry):
            def add(j, carry):
                slot = g * each + j
                into = pl.ds(ids_ref[slot] * units, units)
                piece = incoming_ref[pl.ds(begins_ref[slot], units)].astype(F32)
                sums_ref[into] = sums_ref[into] + piece
                return carry

            return lax.fori_loop(0, filled_ref[g], add, carry)

        lax.fori_loop(0, senders, sender, 0)

        def pack(a, carry):
            piece = sums_ref[pl.ds(a * units, units)]
            sent_ref[pl.ds(spots_ref[a], units)] = piece.astype(BF16)
            return carry

        lax.fori_loop(0, atoms, pack, 0, unroll=4)

    return pl.pallas_call(
        body,
        in_specs=[smem()] * 4 + [pl.BlockSpec(memory_space=pltpu.VMEM)] + unread(after),
        out_specs=[pl.BlockSpec(memory_space=pltpu.VMEM)] * 2,
        out_shape=[
            jax.ShapeDtypeStruct((atoms * units, UNIT, breadth), F32),
            jax.ShapeDtypeStruct((span, UNIT, breadth), BF16),
        ],
        compiler_params=pltpu.CompilerParams(vmem_limit_bytes=GRANT),
        name="merge",
    )(ids, begins, filled, spots, incoming, *after)


def couple(sums, others, high, low, tables, units, room, after):
    breadth = sums.shape[2]
    groups, edge, _ = high.shape
    ids, begins, filled, spots, shared = tables
    senders = filled.shape[0]
    each = ids.shape[0] // senders
    rows = units * UNIT

    def body(ids_ref, begins_ref, filled_ref, spots_ref, shared_ref, sums_ref, others_ref, *refs):
        high_ref, low_ref = refs[:2]
        out_ref, total_ref, kept_ref = refs[2 + len(after) :]

        def mix(g, carry):
            for m in range(GROUP):
                a = g * GROUP + m
                piece = others_ref[pl.ds(spots_ref[a], units)].astype(F32)
                piece = jnp.where(shared_ref[a] > 0, piece, 0.0)
                piece = sums_ref[pl.ds(a * units, units)] + piece
                total_ref[m * rows : (m + 1) * rows] = piece.reshape(rows, breadth)
            total = total_ref[...]
            upper = total.astype(BF16)
            lower = (total - upper.astype(F32)).astype(BF16)
            mixed = jnp.dot(high_ref[g], upper, preferred_element_type=F32)
            mixed = mixed + jnp.dot(low_ref[g], upper, preferred_element_type=F32)
            mixed = mixed + jnp.dot(high_ref[g], lower, preferred_element_type=F32)
            mixed = mixed.reshape(GROUP * units, UNIT, breadth).astype(BF16)
            kept_ref[pl.ds(g * GROUP * units, GROUP * units)] = mixed
            return carry

        lax.fori_loop(0, groups, mix, 0, unroll=4)

        def sender(g, carry):
            def copy(j, carry):
                slot = g * each + j
                piece = kept_ref[pl.ds(ids_ref[slot] * units, units)]
                out_ref[pl.ds(begins_ref[slot], units)] = piece
                return carry

            return lax.fori_loop(0, filled_ref[g], copy, carry)

        lax.fori_loop(0, senders, sender, 0)

    vmem = pl.BlockSpec(memory_space=pltpu.VMEM)
    return pl.pallas_call(
        body,
        in_specs=[smem()] * 5 + [vmem] * 4 + unread(after),
        out_specs=vmem,
        out_shape=jax.ShapeDtypeStruct((room, UNIT, breadth), BF16),
        scratch_shapes=[
            pltpu.VMEM((edge, breadth), F32),
            pltpu.VMEM((sums.shape[0], UNIT, breadth), BF16),
        ],
        compiler_params=pltpu.CompilerParams(vmem_limit_bytes=GRANT),
        name="couple",
    )(ids, begins, filled, spots, shared, sums, others, high, low, *after)


def apply(turned, answers, begun, starts, used, part, cz, per_atom, after):
    cells, nodes, rows = turned.shape
    breadth = answers.shape[2]
    per_cell = rows // per_atom
    units = per_atom // UNIT
    side = begun.shape[2]
    deg = side - 1

    def body(starts_ref, used_ref, turned_ref, answers_ref, begun_ref, *refs):
        total_ref, stack_ref = refs[len(after) :]
        c = pl.program_id(0)

        @pl.when(c == 0)
        def _():
            total_ref[...] = begun_ref[...]

        row = lax.broadcasted_iota(jnp.int32, (per_atom, breadth), 0)
        for k in range(per_cell):
            entry = c * per_cell + k
            piece = answers_ref[pl.ds(starts_ref[entry], units)].astype(F32)
            piece = piece.reshape(per_atom, breadth)
            piece = jnp.where(row < used_ref[entry] * UNIT, piece, 0.0)
            stack_ref[k * per_atom : (k + 1) * per_atom] = piece.astype(BF16)
        result = jnp.dot(turned_ref[0], stack_ref[...], preferred_element_type=F32)
        u = pl.ds(c // cz * deg, side)
        w = pl.ds(c % cz * deg, side)
        total_ref[u, w] = total_ref[u, w] + result.reshape(side, side, side, breadth)

    shape = begun.shape[:3] + (breadth,)
    return pl.pallas_call(
        body,
        grid=(cells,),
        in_specs=[
            smem(),
            smem(),
            pl.BlockSpec((1, nodes, rows), lambda c: (c, 0, 0)),
            whole(answers.shape),
            pl.BlockSpec(shape, lambda c: (0, 0, 0, part), pipeline_mode=pl.Buffered(1)),
        ]
        + unread(after),
        out_specs=whole(shape),
        out_shape=jax.ShapeDtypeStruct(shape, F32),
        scratch_shapes=[pltpu.VMEM((rows, breadth), BF16)],
        compiler_params=pltpu.CompilerParams(vmem_limit_bytes=GRANT),
        name="apply",
    )(starts, used, turned, answers, begun, *after)


def finish(total, sides, ends, scale, older):
    span_u, span_w, span_v, breadth = total.shape

    def body(scale_ref, total_ref, prev_v_ref, next_v_ref, prev_u_ref, next_u_ref, *refs):
        out_ref = refs[-1]
        times = scale_ref[0]
        at = lax.broadcasted_iota(jnp.int32, (span_w, span_v, breadth), 1)

        def row(u, carry):
            first = prev_v_ref[u].astype(F32)[:, None]
            last = next_v_ref[u].astype(F32)[:, None]
            value = total_ref[u] + jnp.where(at == 0, first, 0.0)
            value = times * (value + jnp.where(at == span_v - 1, last, 0.0))
            if older is not None:
                value = value - refs[0][u]
            out_ref[u] = value
            return carry

        lax.fori_loop(0, span_u, row, 0)
        out_ref[0] = out_ref[0] + times * prev_u_ref[...].astype(F32)
        out_ref[span_u - 1] = out_ref[span_u - 1] + times * next_u_ref[...].astype(F32)

    vmem = pl.BlockSpec(memory_space=pltpu.VMEM)
    known = [] if older is None else [older]
    return pl.pallas_call(
        body,
        in_specs=[smem()] + [vmem] * (5 + len(known)),
        out_specs=vmem,
        out_shape=jax.ShapeDtypeStruct(total.shape, F32),
        compiler_params=pltpu.CompilerParams(vmem_limit_bytes=GRANT),
        name="finish",
    )(scale, total, *sides, *ends, *known)


def completed(total, scale, older, final):
    prev_v = shifted(total[:, :, -1].astype(BF16), ("gy",), (1,))
    next_v = prev_v if final else shifted(total[:, :, 0].astype(BF16), ("gy",), (-1,))

    def edge(u):
        row = total[u]
        first = row[:, :1] + prev_v[u][:, None].astype(F32)
        last = row[:, -1:] + next_v[u][:, None].astype(F32)
        return jnp.concatenate([first, row[:, 1:-1], last], axis=1).astype(BF16)

    prev_u = shifted(edge(-1), ("gx",), (1,))
    next_u = prev_u if final else shifted(edge(0), ("gx",), (-1,))
    return finish(total, (prev_v, next_v), (prev_u, next_u), scale, older)


def on_device(orbitals, cell_matrices, cell_nodes, projectors, entry_atom, coupling, proj_counts):
    span_x, span_y, layers, _ = orbitals.shape
    matrices = cell_matrices[0, 0]
    node_map = cell_nodes[0, 0]
    cells, per_cell, per_atom, nodes = projectors.shape[2:]
    shapes = projectors[0, 0].reshape(cells, per_cell * per_atom, nodes)
    atom_names = entry_atom[0, 0]
    side = round(nodes ** (1 / 3))
    deg = side - 1
    cz = (layers - 1) // deg
    assert span_y == deg and side**3 == nodes and cells * deg == span_x * cz
    entries = cells * per_cell
    n_gx, n_gy = lax.axis_size("gx"), lax.axis_size("gy")
    devices = n_gx * n_gy
    half = n_gy // 2
    senders = devices // 2
    home_atoms = coupling.shape[0]
    atoms = 2 * home_atoms
    each = 2 * max(2, 2 * entries // devices)
    slots = senders * each
    both = ("gx", "gy")
    teams = [
        [p * n_gy + h * half + r for p in range(n_gx) for r in range(half)] for h in range(2)
    ]

    def exchange(x):
        return lax.all_to_all(
            x, both, split_axis=0, concat_axis=0, axis_index_groups=teams, tiled=True
        )

    units = per_atom // UNIT
    my_x, my_y = lax.axis_index("gx"), lax.axis_index("gy")
    my_half, my_place = my_y // half, my_y % half
    me = my_x * n_gy + my_y
    mine = my_x * half + my_place

    notes = jnp.concatenate([atom_names.reshape(entries), proj_counts])
    notes = jnp.broadcast_to(notes, (devices, entries + home_atoms))
    notes = lax.all_to_all(notes, both, split_axis=0, concat_axis=0, tiled=True)
    names, counts = notes[:, :entries], notes[:, entries:]
    needs = (counts + UNIT - 1) // UNIT
    homes, inner = names // home_atoms, names % home_atoms
    homes_y = homes % n_gy
    at_home = (homes[:, :, None] == jnp.arange(devices)).astype(BF16)
    at_inner = (inner[:, :, None] == jnp.arange(home_atoms)).astype(BF16)
    picked = jnp.einsum("seh,hi->sei", at_home, needs.astype(BF16), preferred_element_type=F32)
    sizes = jnp.sum(picked * at_inner.astype(F32), axis=2).astype(jnp.int32)

    def by_half(x):
        return x.reshape((n_gx, 2, half) + x.shape[1:])

    split = [
        jnp.einsum(
            "seh,sei->hi",
            by_half(at_home)[:, h].reshape((senders,) + at_home.shape[1:]),
            by_half(at_inner)[:, h].reshape((senders,) + at_inner.shape[1:]),
            preferred_element_type=F32,
        )
        for h in range(2)
    ]
    common = ((split[0] > 0) & (split[1] > 0)).astype(jnp.int32)

    order = jnp.arange(entries)[None, :, None]
    present = homes[:, :, None] == jnp.arange(devices)
    sized = sizes[:, :, None]
    loads = jnp.sum(jnp.where(present, sized, 0), axis=1)
    ends = jnp.max(jnp.where(present, order * (2 * units) + sized, 0), axis=1)
    crossing = jnp.sum(common * needs, axis=1)
    table = jnp.concatenate([loads, ends, crossing[None]], axis=0).astype(F32)
    table = table.reshape(2 * devices + 1, n_gx, 2, half)
    lower = table[:, :, 0].reshape(-1, 1, senders)
    turned_to = np.zeros((senders, TURNS * TURNS, senders), np.float32)
    for j, k, p, r in itertools.product(range(TURNS), range(TURNS), range(n_gx), range(half)):
        source = (p + j) % n_gx * half + (r + k) % half
        turned_to[source, j * TURNS + k, p * half + r] = 1.0
    upper = jnp.einsum(
        "ah,hcg->acg",
        table[:, :, 1].reshape(-1, senders),
        jnp.asarray(turned_to),
        precision=lax.Precision.HIGHEST,
    )
    tail = jnp.maximum(lower, upper)[devices : 2 * devices].astype(jnp.int32) % (2 * units)
    joint = (lower + upper).astype(jnp.int32)
    cap = TIGHT * each * units // 64
    span = NARROW * atoms * units // 256
    fullest = jnp.max(joint[:devices] - tail + units, axis=(0, 2))
    widest = jnp.max(joint[-1] + units, axis=1)
    scores = jnp.maximum(fullest * span, widest * cap)
    best = jnp.argmin(scores).astype(jnp.int32)
    fits = jnp.min(scores) <= cap * span
    turn_x, turn_y = best // TURNS, best % TURNS
    over = homes_y // half
    held = over * home_atoms + inner
    places_x = (homes // n_gy - turn_x * over) % n_gx
    places_y = (homes_y % half - turn_y * over) % half
    collectors = places_x * half + places_y

    def of_me(x):
        return lax.dynamic_index_in_dim(x, me, 0, keepdims=False)

    def of_my_half(x):
        x = lax.dynamic_index_in_dim(by_half(x), my_half, 1, keepdims=False)
        return x.reshape((senders,) + x.shape[2:])

    def hosted(x):
        first = my_x * n_gy + my_place
        second = (my_x + turn_x) % n_gx * n_gy + half + (my_place + turn_y) % half
        rows = [lax.dynamic_index_in_dim(x, at, 0, keepdims=False) for at in (first, second)]
        return jnp.concatenate(rows)

    before = jnp.arange(entries)[:, None] < jnp.arange(entries)[None, :]
    own, used = of_me(collectors), of_me(sizes)
    ahead = before & (own[:, None] == own[None, :])
    offsets = jnp.sum(jnp.where(ahead, used[:, None], 0), axis=0)
    theirs = (of_my_half(collectors) == mine).astype(BF16)
    earlier = before.astype(BF16)
    ranks = jnp.dot(theirs, earlier, preferred_element_type=F32).astype(jnp.int32)
    lengths = theirs * of_my_half(sizes).astype(BF16)
    shifts = jnp.dot(lengths, earlier, preferred_element_type=F32).astype(jnp.int32)
    chosen = (ranks[:, None, :] == jnp.arange(each)[:, None]) & (theirs[:, None, :] > 0)
    ids = jnp.sum(jnp.where(chosen, of_my_half(held)[:, None, :], 0), axis=2).reshape(slots)
    places_in = jnp.sum(jnp.where(chosen, shifts[:, None, :], 0), axis=2)
    filled = jnp.sum(theirs.astype(F32), axis=1).astype(jnp.int32)
    shared = hosted(common)
    moved = shared * hosted(needs)
    upto = jnp.arange(atoms)[:, None] < jnp.arange(atoms)[None, :]
    spots = jnp.sum(jnp.where(upto, moved[:, None], 0), axis=0)

    flat = coupling.reshape(-1, 128)
    partner = shifted(flat, ("gy",), (half,))
    lower_mix = jnp.where(my_half > 0, partner, flat)
    upper_mix = jnp.where(my_half > 0, flat, partner)
    choices = [upper_mix] + [shifted(upper_mix, ("gx",), (-j,)) for j in range(1, TURNS)]
    upper_mix = lax.select_n(turn_x, *choices)
    choices = [upper_mix]
    for k in range(1, TURNS):
        pairs = [(h * half + (r + k) % half, h * half + r) for h in range(2) for r in range(half)]
        choices.append(lax.ppermute(upper_mix, "gy", pairs))
    upper_mix = lax.select_n(turn_y, *choices)
    mixers = jnp.concatenate([lower_mix, upper_mix], axis=0).reshape(atoms, per_atom, per_atom)
    active = (jnp.arange(per_atom)[None, :] < hosted(counts)[:, None]).astype(F32)
    mixers = mixers * active[:, :, None] * active[:, None, :]

    cell_ids = jnp.arange(cells, dtype=jnp.int32)[:, None]
    node_w = node_map % layers - cell_ids % cz * deg
    node_v = node_map // layers % (span_y + 1)
    node_u = node_map // (layers * (span_y + 1)) - cell_ids // cz * deg
    places = (node_u * side + node_w) * side + node_v
    places = places.reshape(cells, 1, nodes)

    row_next = shifted(orbitals[0], ("gx",), (-1,))[None]
    column_next = shifted(orbitals[:, 0], ("gy",), (-1,))[:, None]
    corner_next = shifted(orbitals[0, 0], both, (-1, -1))[None, None]
    widened = jnp.concatenate(
        [
            jnp.concatenate([orbitals, column_next], axis=1),
            jnp.concatenate([row_next, corner_next], axis=1),
        ],
        axis=0,
    )
    grid = jnp.transpose(widened, (0, 2, 1, 3)).astype(F32)
    extended = grid.shape[:3]

    def advance(field, older, scale, known, cap, span, final=False):
        room = senders * cap
        starts = own * cap + offsets
        begins = (places_in + jnp.arange(senders)[:, None] * cap).reshape(slots)
        tables = (ids, begins, filled, spots, shared)
        if known is None:
            straight, local, *outgoing = project(field, shapes, starts, room, cz, per_atom, places)
        else:
            straight, stiff, turned, *mixing = known
            local, *outgoing = project(field, straight, starts, room, cz, per_atom)
        if known is None:
            stiff, turned = canonical(places, matrices, shapes, (local,))
            mixing = spread(mixers, (turned,))
        image = stiffen(stiff, local, extended, cz)
        after = ()
        gathered = []
        for packet in outgoing:
            incoming = exchange(packet)
            gathered.append(merge(incoming, tables, atoms, units, span, after))
            after = (gathered[-1][0],)
        after = after + (image,)
        answers = []
        for sums, sent in gathered:
            others = shifted(sent, ("gy",), (half,))
            replies = couple(sums, others, *mixing, tables, units, room, after)
            answers.append(exchange(replies))
            after = (replies,)
        totals = []
        for part in range(PARTS):
            totals.append(
                apply(turned, answers[part], image, starts, used, part, cz, per_atom, after)
            )
            after = (totals[-1],)
        total = jnp.concatenate(totals, axis=-1) if PARTS > 1 else totals[0]
        return completed(total, scale, older, final), (straight, stiff, turned, *mixing)

    def packed():
        known = None
        older, field = None, grid
        for step in range(FILTER_DEGREE):
            scale = jnp.full((1,), 1.0 if step == 0 else 2.0, F32)
            final = step == FILTER_DEGREE - 1
            image, known = advance(field, older, scale, known, cap, span, final)
            older, field = field, image
        return field[:span_x, :, :span_y].astype(BF16)

    def roomy():
        def step(at, fields):
            older, field = fields
            scale = jnp.where(at == 0, 1.0, 2.0).astype(F32).reshape(1)
            image, _ = advance(
                field, older, scale, None, (each + 1) * units, (atoms + 1) * units
            )
            return field, image

        fields = (jnp.zeros_like(grid), grid)
        field = lax.fori_loop(0, FILTER_DEGREE, step, fields)[1]
        return field[:span_x, :, :span_y].astype(BF16)

    if MODE == "cond":
        filtered = lax.cond(fits, packed, roomy)
    else:
        filtered = packed() if MODE == "fast" else roomy()
    return jnp.transpose(filtered, (0, 2, 1, 3))


def solution(mesh):
    in_specs = (
        P("gx", "gy", None, None),
        P("gx", "gy", None, None, None),
        P("gx", "gy", None, None),
        P("gx", "gy", None, None, None, None),
        P("gx", "gy", None, None),
        P(("gx", "gy"), None, None),
        P(("gx", "gy")),
    )
    out_specs = P("gx", "gy", None, None)
    return jax.shard_map(
        on_device, mesh=mesh, in_specs=in_specs, out_specs=out_specs, check_vma=False
    )
```
